32 devices in a mesh: member: 2 (over x), gx: 16 (over z, y, core).
Axes of the slice: x: 2, y: 2, z: 4, core: 2. Of those that a mesh axis runs over, the one named last changes fastest.
Arguments:
- analysis: bfloat16 [3, 4, 1536, 512], P(None, None, 'gx'), may hold values from -4 to 4
- zonal_waves: int32 [8, 16], P('member'), parts along dimension 0, may hold values from 0 to 511
- meridional_waves: int32 [8, 16], P('member'), parts along dimension 0, may hold values from 0 to 1535
- amplitude_codes: int32 [8, 16], P('member'), parts along dimension 0, may hold values from 1 to 8
Outputs:
- forecast: bfloat16 [6, 4, 512, 1536], P('member', None, 'gx'), parts along dimension 0
The draws below stay inside these ranges and needn't reach their ends.
There are 2 independent parts, one for each index of `member`. The reference program is written for one: setup_inputs(seed, part) draws one part's arguments, and reference() takes and returns one part's arrays. A program takes and returns all parts, laid end to end along the dimension named above; an argument that names none is the same for every part. Nothing has to cross between parts.
All inputs are finite; a program needn't handle non-finite values.
Results may differ from the reference program's by a relative error of at most 0.006.
Values may be sent and summed in bfloat16 or wider, within the bound.
No kernel may reach another device: no remote copies, remote signals or barrier semaphores. Data moves between devices by JAX's collectives and lax.ppermute only.
A program may use at most 64 MiB of HBM per device.

```python
import math
import jax
import jax.numpy as jnp
from jax import lax

NY = 1536
LEV = 4
MODES = 16
STEPS = 4
NX = 512


def with_ends(entries, key, low, top_value):
    place = [jax.random.randint(jax.random.fold_in(key, axis), (), 0, length) for axis, length in enumerate(entries.shape)]
    main_axis = entries.shape.index(max(entries.shape))
    beside = place[:main_axis] + [(place[main_axis] + 1) % entries.shape[main_axis]] + place[main_axis + 1:]
    return entries.at[tuple(place)].set(low).at[tuple(beside)].set(top_value)


def levels(stream_key, dims, pieces, smallest, high):
    def one(position, blocks):
        steps = jax.random.uniform(jax.random.fold_in(jax.random.fold_in(stream_key, 6), position), (blocks,), jnp.float32, smallest / len(pieces), high / len(pieces))
        return jnp.repeat(jnp.exp(steps), dims[position] // blocks).reshape((-1,) + (1,) * (len(dims) - position - 1))

    factor_of = one(*pieces[0])
    for cut in pieces[1:]:
        factor_of = factor_of * one(*cut)
    return factor_of


def normal_values(stream_key, dims, scale, most, split=(), kind=jnp.bfloat16):
    values = jax.random.normal(stream_key, dims, jnp.float32) * scale
    if len(split) > 0:
        values = levels(stream_key, dims, split, -0.22, 0.18) * values
    return jnp.clip(values, min=-most, max=most).astype(kind)


def setup_inputs(seed: int = 0, part: int = 0) -> dict:
    splits = jax.random.split(jax.random.key(seed), 5)
    part_splits = jax.random.split(jax.random.fold_in(splits[4], part), 5)
    analysis = normal_values(splits[0], (3, LEV, NY, NX), 0.5, 4.0, ((2, 16),))
    zonal_waves = with_ends(jax.random.randint(part_splits[1], (LEV, MODES), 0, NX), jax.random.fold_in(part_splits[1], 1), 0, NX - 1).astype(jnp.int32)
    meridional_waves = with_ends(jax.random.randint(part_splits[2], (LEV, MODES), 0, NY), jax.random.fold_in(part_splits[2], 1), 0, NY - 1).astype(jnp.int32)
    amplitude_codes = with_ends(jax.random.randint(part_splits[3], (LEV, MODES), 1, 9), jax.random.fold_in(part_splits[3], 1), 1, 8).astype(jnp.int32)
    return {"analysis": analysis, "zonal_waves": zonal_waves, "meridional_waves": meridional_waves, "amplitude_codes": amplitude_codes}


TIME_STEP = 0.15
FILTER = 0.03
GRAVITY = 0.5
AMP_UNIT = 0.04


def take_cells(values, axis_dim, offset, length):
    return lax.slice_in_dim(values, offset, offset + length, axis=axis_dim)


def centred(quantity, axis_dim, length):
    near_pair = take_cells(quantity, axis_dim, 3, length) - take_cells(quantity, axis_dim, 1, length)
    far_pair = take_cells(quantity, axis_dim, 4, length) - take_cells(quantity, axis_dim, 0, length)
    return (8.0 * near_pair - far_pair) * (1.0 / 12.0)


def fourth(quantity, axis_dim, length):
    outer = take_cells(quantity, axis_dim, 0, length) + take_cells(quantity, axis_dim, 4, length)
    inner = take_cells(quantity, axis_dim, 1, length) + take_cells(quantity, axis_dim, 3, length)
    return outer - 4.0 * inner + 6.0 * take_cells(quantity, axis_dim, 2, length)


def advance(padded, lon_dim, lat_dim, lat_rows, lat_total):
    fields = padded.astype(jnp.float32)
    thickness, eastward, northward = fields[0], fields[1], fields[2]
    lon_axis = lon_dim - 1
    lat_axis = lat_dim - 1
    lon_count = thickness.shape[lon_axis] - 4
    lat_count = thickness.shape[lat_axis] - 4
    latitude = (math.pi / 3.0) * (2.0 * (lat_rows.astype(jnp.float32) + 0.5) / lat_total - 1.0)
    layout_shape = [1, 1, 1]
    layout_shape[lat_axis] = lat_count
    inverse = (1.0 / jnp.cos(latitude)).reshape(layout_shape)
    coriolis = (2.0 * jnp.sin(latitude)).reshape(layout_shape)
    pressure = GRAVITY * (0.5 * jnp.sum(thickness, axis=0, keepdims=True) + 0.5 * lax.cumsum(thickness, axis=0, reverse=True))

    def strip_lon(quantity):
        return take_cells(quantity, lat_axis, 2, lat_count)

    def strip_lat(quantity):
        return take_cells(quantity, lon_axis, 2, lon_count)

    def slope_lon(quantity):
        return centred(strip_lon(quantity), lon_axis, lon_count) * inverse

    def slope_lat(quantity):
        return centred(strip_lat(quantity), lat_axis, lat_count)

    def smooth(quantity):
        return fourth(strip_lon(quantity), lon_axis, lon_count) + fourth(strip_lat(quantity), lat_axis, lat_count)

    column = 1.0 + thickness
    thick_mid = strip_lon(strip_lat(thickness))
    east_mid = strip_lon(strip_lat(eastward))
    north_mid = strip_lon(strip_lat(northward))
    thick_tend = -(slope_lon(column * eastward) + slope_lat(column * northward))
    east_tend = -(east_mid * slope_lon(eastward) + north_mid * slope_lat(eastward)) - slope_lon(pressure) + coriolis * north_mid
    north_tend = -(east_mid * slope_lon(northward) + north_mid * slope_lat(northward)) - slope_lat(pressure) - coriolis * east_mid
    thick_new = thick_mid + TIME_STEP * thick_tend - FILTER * smooth(thickness)
    east_new = east_mid + TIME_STEP * east_tend - FILTER * smooth(eastward)
    north_new = north_mid + TIME_STEP * north_tend - FILTER * smooth(northward)
    return jnp.stack([thick_new, east_new, north_new], axis=0).astype(jnp.bfloat16)


def perturbation(lon_cells, lat_cells, zonal_waves, meridional_waves, amplitude_codes, lon_total, lat_total, lat_first):
    lon_phase = ((lon_cells[None, :, None] * zonal_waves[:, None, :]) % lon_total).astype(jnp.float32) * (2.0 * math.pi / lon_total)
    lat_phase = ((lat_cells[None, :, None] * meridional_waves[:, None, :]) % lat_total).astype(jnp.float32) * (2.0 * math.pi / lat_total)
    weights = (AMP_UNIT * amplitude_codes.astype(jnp.float32))[:, None, :]
    left_table = jnp.concatenate([weights * jnp.cos(lon_phase), -weights * jnp.sin(lon_phase)], axis=2)
    right_table = jnp.concatenate([jnp.cos(lat_phase), jnp.sin(lat_phase)], axis=2)
    if lat_first:
        return jnp.einsum("lym,lxm->lyx", right_table, left_table, precision=lax.Precision.HIGHEST)
    return jnp.einsum("lxm,lym->lxy", left_table, right_table, precision=lax.Precision.HIGHEST)


def reference(analysis, zonal_waves, meridional_waves, amplitude_codes):
    columns = jnp.transpose(analysis, (0, 1, 3, 2))
    lon_total = analysis.shape[3]
    lat_total = analysis.shape[2]
    lon_cells = jnp.arange(lon_total, dtype=jnp.int32)
    lat_cells = jnp.arange(lat_total, dtype=jnp.int32)
    added = perturbation(lon_cells, lat_cells, zonal_waves, meridional_waves, amplitude_codes, lon_total, lat_total, False)
    thickness = (columns[0].astype(jnp.float32) + added).astype(jnp.bfloat16)
    state = jnp.concatenate([thickness[None], columns[1:]], axis=0)
    for turn_index in range(STEPS):
        wrapped = jnp.concatenate([state[:, :, -2:], state, state[:, :, :2]], axis=2)
        padded = jnp.pad(wrapped, ((0, 0), (0, 0), (0, 0), (2, 2)))
        state = advance(padded, 2, 3, lat_cells, lat_total)
    return state
```

```python
import functools
import math

import jax
import jax.numpy as jnp
from jax import lax
from jax.experimental import pallas as pl
from jax.experimental.pallas import tpu as pltpu
from jax.sharding import PartitionSpec as P

NY = 1536
STEPS = 4
TIME_STEP = 0.15
FILTER = 0.03
GRAVITY = 0.5
AMP_UNIT = 0.04
LANES = 128
SUBS = 8
MARGIN = 2 * STEPS


def lon_shifts(x, halves, lane):
    ahead = pltpu.roll(x, SUBS - halves, 0)
    behind = pltpu.roll(x, halves, 0)
    return (
        pltpu.roll(jnp.where(lane < 1, ahead, x), LANES - 1, 1),
        pltpu.roll(jnp.where(lane >= LANES - 1, behind, x), 1, 1),
        pltpu.roll(jnp.where(lane < 2, ahead, x), LANES - 2, 1),
        pltpu.roll(jnp.where(lane >= LANES - 2, behind, x), 2, 1),
    )


def slope(p1, m1, p2, m2):
    return 8.0 * (p1 - m1) - (p2 - m2)


def level_sums(slopes):
    below = [None] * len(slopes)
    running = None
    for k in reversed(range(len(slopes))):
        running = slopes[k] if running is None else running + slopes[k]
        below[k] = running
    return [(0.5 * GRAVITY) * (running + b) for b in below]


def step_rows(src, dst, coef, first, count, halves, levels):
    lane = lax.broadcasted_iota(jnp.int32, (SUBS, LANES), 1)
    cy = TIME_STEP / 12.0
    loaded = {}

    def get(f, k):
        if (f, k) not in loaded:
            start = pl.multiple_of((first + k) * SUBS, SUBS)
            loaded[f, k] = src[f, pl.ds(start, SUBS), :]
        return loaded[f, k]

    flux = {}

    def north_flux(l, k):
        if (l, k) not in flux:
            v = get(2 * levels + l, k)
            flux[l, k] = v + get(l, k) * v
        return flux[l, k]

    for k in range(count):
        start = pl.multiple_of((first + k) * SUBS, SUBS)
        rx = coef[0, pl.ds(start, SUBS), :]
        fc = coef[1, pl.ds(start, SUBS), :]
        ax, ay, smooth = {}, {}, {}
        for c in range(3):
            for l in range(levels):
                f = c * levels + l
                q = get(f, k)
                xp1, xm1, xp2, xm2 = lon_shifts(q, halves, lane)
                yp1, ym1, yp2, ym2 = get(f, k + 1), get(f, k - 1), get(f, k + 2), get(f, k - 2)
                ax[c, l] = slope(xp1, xm1, xp2, xm2)
                ay[c, l] = slope(yp1, ym1, yp2, ym2)
                near = (xp1 + xm1) + (yp1 + ym1)
                far = (xp2 + xm2) + (yp2 + ym2)
                smooth[c, l] = (1.0 - 12.0 * FILTER) * q + FILTER * (4.0 * near - far)
        apx = level_sums([ax[0, l] for l in range(levels)])
        apy = level_sums([ay[0, l] for l in range(levels)])
        for l in range(levels):
            h, u, v = get(l, k), get(levels + l, k), get(2 * levels + l, k)
            east = slope(*lon_shifts(u + h * u, halves, lane))
            north = slope(north_flux(l, k + 1), north_flux(l, k - 1), north_flux(l, k + 2), north_flux(l, k - 2))
            h_new = smooth[0, l] - (rx * east + cy * north)
            u_new = smooth[1, l] - rx * (u * ax[1, l] + apx[l]) - v * (cy * ay[1, l] - fc)
            v_new = smooth[2, l] - u * (rx * ax[2, l] + fc) - cy * (v * ay[2, l] + apy[l])
            dst[l, pl.ds(start, SUBS), :] = h_new
            dst[levels + l, pl.ds(start, SUBS), :] = u_new
            dst[2 * levels + l, pl.ds(start, SUBS), :] = v_new


UNROLL = 4


def member_kernel(levels, halves, blocks, place_ref, own_ref, low_ref, high_ref, lat_ref, lon_ref, coef_ref, *rest):
    outs, (one, two, coef, ready) = rest[: -4], rest[-4:]
    rows = own_ref.shape[2]
    half_rows = rows // halves
    length = half_rows + 2 * MARGIN
    place = place_ref[0]

    for which in range(2):
        for t in range(length):
            coef[which, t * SUBS : (t + 1) * SUBS, :] = jnp.broadcast_to(coef_ref[which, :, t : t + 1], (SUBS, LANES))

    def load(l, carry):
        added = lax.dot_general(
            lat_ref[l], lon_ref[l], (((0,), (0,)), ((), ())),
            precision=lax.Precision.HIGHEST, preferred_element_type=jnp.float32,
        )
        for c in range(3):
            whole = jnp.concatenate(
                [r[c, l].astype(jnp.float32) for r in (low_ref, own_ref, high_ref)], axis=0
            )
            if c == 0:
                whole = (whole + added[: rows + 2 * MARGIN]).astype(jnp.bfloat16).astype(jnp.float32)
            for half in range(halves):
                for b in range(blocks):
                    for t in range(0, length, SUBS):
                        at = half * half_rows + t
                        one[c * levels + l, pl.ds(t * SUBS + b * halves + half, SUBS, stride=SUBS), :] = whole[
                            at : at + SUBS, b * LANES : (b + 1) * LANES
                        ]
        return carry

    lax.fori_loop(0, levels, load, 0)

    src, dst = one, two
    for step in range(STEPS):
        begin = 2 * (step + 1)
        count = length - 2 * begin

        def body(i, carry, src=src, dst=dst, begin=begin):
            step_rows(src, dst, coef, begin + i * UNROLL, UNROLL, halves, levels)
            return carry

        lax.fori_loop(0, count // UNROLL, body, 0)
        if step < STEPS - 1:
            @pl.when((place_ref[1] == 0) | (place_ref[1] == place_ref[2] - 1))
            def _(dst=dst, begin=begin):
                def clear(f, carry):
                    for t in list(range(begin, MARGIN)) + list(range(length - MARGIN, length - begin)):
                        inside = coef_ref[2, :, t : t + 1] > 0.5
                        at = slice(t * SUBS, (t + 1) * SUBS)
                        dst[f, at, :] = jnp.where(inside, dst[f, at, :], 0.0)
                    return carry

                lax.fori_loop(0, 3 * levels, clear, 0)
        src, dst = dst, src

    total = levels * rows
    per = len(outs)
    width = blocks * LANES // per
    for c in range(3):
        for b in range(blocks):
            tiles = []
            for l in range(levels):
                for half in range(halves):
                    for t in range(MARGIN, MARGIN + half_rows, SUBS):
                        tiles.append(src[c * levels + l, pl.ds(t * SUBS + b * halves + half, SUBS, stride=SUBS), :])
            for j in range(total // LANES):
                square = jnp.concatenate(tiles[j * (LANES // SUBS) : (j + 1) * (LANES // SUBS)], axis=0)
                turned = square.T.astype(jnp.bfloat16)
                for d in range(LANES // width):
                    ready[b * (LANES // width) + d, c, :, j * LANES : (j + 1) * LANES] = turned[d * width : (d + 1) * width]
    for k in range(per):
        outs[k][...] = ready[place_ref[3 + k]]


def gather_kernel(levels, rows, place_ref, *refs):
    ins, out_ref, held = refs[:-2], refs[-2], refs[-1]
    n = len(ins)
    for k in range(n):
        held[place_ref[3 + k]] = ins[k][...]
    width = ins[0].shape[1]
    for c in range(3):
        for l in range(levels):
            out_ref[c, l] = jnp.concatenate(
                [held[s, c, :, l * rows : (l + 1) * rows] for s in range(n)], axis=1
            )


def shards(analysis, zonal_waves, meridional_waves, amplitude_codes):
    n = lax.axis_size("gx")
    place = lax.axis_index("gx")
    _, levels, rows, lon_total = analysis.shape
    lat_total = rows * n
    blocks = lon_total // LANES
    halves = SUBS // blocks
    half_rows = rows // halves
    length = half_rows + 2 * MARGIN
    width = lon_total // n
    total = levels * rows

    ahead = [(i, i + 1) for i in range(n - 1)]
    back = [(i + 1, i) for i in range(n - 1)]
    low = lax.ppermute(analysis[:, :, rows - MARGIN :], "gx", ahead)
    high = lax.ppermute(analysis[:, :, :MARGIN], "gx", back)

    modes = zonal_waves.shape[1]
    lon_cells = jnp.arange(lon_total, dtype=jnp.int32)
    lon_phase = (lon_cells[None, None, :] * zonal_waves[:, :, None] % lon_total).astype(jnp.float32) * (
        2.0 * math.pi / lon_total
    )
    weights = (AMP_UNIT * amplitude_codes.astype(jnp.float32))[:, :, None]
    lon_table = jnp.concatenate([weights * jnp.cos(lon_phase), -weights * jnp.sin(lon_phase)], axis=1)
    padded = -(-(rows + 2 * MARGIN) // LANES) * LANES
    lat_cells = place * rows - MARGIN + jnp.arange(padded, dtype=jnp.int32)
    inside = (lat_cells >= 0) & (lat_cells < lat_total)
    lat_phase = (lat_cells[None, None, :] * meridional_waves[:, :, None] % lat_total).astype(jnp.float32) * (
        2.0 * math.pi / lat_total
    )
    lat_table = jnp.concatenate([jnp.cos(lat_phase), jnp.sin(lat_phase)], axis=1)
    lat_table = jnp.where(inside[None, None, :], lat_table, 0.0)

    half_of = jnp.arange(SUBS, dtype=jnp.int32) % halves
    cell = place * rows - MARGIN + half_of[:, None] * half_rows + jnp.arange(length, dtype=jnp.int32)[None, :]
    latitude = math.pi / 3.0 * (2.0 * (cell.astype(jnp.float32) + 0.5) / lat_total - 1.0)
    valid = (cell >= 0) & (cell < lat_total)
    factor = (TIME_STEP / 12.0) / jnp.cos(latitude)
    turning = (2.0 * TIME_STEP) * jnp.sin(latitude)
    coef = jnp.stack([factor, turning, valid.astype(jnp.float32)])

    order = jnp.arange(n, dtype=jnp.int32) ^ place
    scalars = jnp.concatenate([jnp.stack([place, place, jnp.int32(n)]).astype(jnp.int32), order])

    vmem = pl.BlockSpec(memory_space=pltpu.VMEM)
    smem = pl.BlockSpec(memory_space=pltpu.SMEM)
    piece = jax.ShapeDtypeStruct((3, width, total), jnp.bfloat16)
    sent = pl.pallas_call(
        functools.partial(member_kernel, levels, halves, blocks),
        out_shape=[piece] * n,
        in_specs=[smem] + [vmem] * 6,
        out_specs=[vmem] * n,
        scratch_shapes=[
            pltpu.VMEM((3 * levels, length * SUBS, LANES), jnp.float32),
            pltpu.VMEM((3 * levels, length * SUBS, LANES), jnp.float32),
            pltpu.VMEM((2, length * SUBS, LANES), jnp.float32),
            pltpu.VMEM((n, 3, width, total), jnp.bfloat16),
        ],
        compiler_params=pltpu.CompilerParams(vmem_limit_bytes=56 * 1024 * 1024),
        name="member_steps",
    )(scalars, analysis, low, high, lat_table, lon_table, coef)

    got = [None] * n
    got[0] = sent[0]
    for k in reversed(range(1, n)):
        got[k] = lax.ppermute(sent[k], "gx", [(i, i ^ k) for i in range(n)])
    return pl.pallas_call(
        functools.partial(gather_kernel, levels, rows),
        out_shape=jax.ShapeDtypeStruct((3, levels, width, lat_total), jnp.bfloat16),
        in_specs=[smem] + [vmem] * n,
        out_specs=vmem,
        scratch_shapes=[pltpu.VMEM((n, 3, width, total), jnp.bfloat16)],
        compiler_params=pltpu.CompilerParams(vmem_limit_bytes=48 * 1024 * 1024),
        name="lay_out",
    )(scalars, *got)


def solution(mesh):
    placed = (P(None, None, "gx", None), P("member", None), P("member", None), P("member", None))
    return jax.shard_map(
        shards, mesh=mesh, in_specs=placed, out_specs=P("member", None, "gx", None), check_vma=False
    )
```

```python
import functools
import math

import jax
import jax.numpy as jnp
from jax import lax
from jax.experimental import pallas as pl
from jax.experimental.pallas import tpu as pltpu
from jax.sharding import PartitionSpec as P

NY = 1536
STEPS = 4
TIME_STEP = 0.15
FILTER = 0.03
GRAVITY = 0.5
AMP_UNIT = 0.04
LANES = 128
SUBS = 16
TILE = 8
MARGIN = 2 * STEPS


def lon_shifts(x, halves, lane):
    ahead = pltpu.roll(x, SUBS - halves, 0)
    behind = pltpu.roll(x, halves, 0)
    return (
        pltpu.roll(jnp.where(lane < 1, ahead, x), LANES - 1, 1),
        pltpu.roll(jnp.where(lane >= LANES - 1, behind, x), 1, 1),
        pltpu.roll(jnp.where(lane < 2, ahead, x), LANES - 2, 1),
        pltpu.roll(jnp.where(lane >= LANES - 2, behind, x), 2, 1),
    )


def slope(p1, m1, p2, m2):
    return 8.0 * (p1 - m1) - (p2 - m2)


def level_sums(slopes):
    below = [None] * len(slopes)
    running = None
    for k in reversed(range(len(slopes))):
        running = slopes[k] if running is None else running + slopes[k]
        below[k] = running
    return [(0.5 * GRAVITY) * (running + b) for b in below]


def rows_of(ref, f, t):
    return ref[f, pl.ds(pl.multiple_of(t * SUBS, SUBS), SUBS), :]


def step_rows(src, dst, coef, first, count, halves, levels):
    lane = lax.broadcasted_iota(jnp.int32, (SUBS, LANES), 1)
    gy = TIME_STEP / 12.0 / FILTER
    loaded = {}

    def get(f, k):
        if (f, k) not in loaded:
            loaded[f, k] = rows_of(src, f, first + k).astype(jnp.bfloat16)
        return loaded[f, k]

    flux = {}

    def north_flux(l, k):
        if (l, k) not in flux:
            v = get(2 * levels + l, k)
            flux[l, k] = v + get(l, k) * v
        return flux[l, k]

    def parts(c, l, k):
        q = get(c * levels + l, k)
        xp1, xm1, xp2, xm2 = lon_shifts(q, halves, lane)
        yp1, ym1, yp2, ym2 = (get(c * levels + l, k + d) for d in (1, -1, 2, -2))
        ax = slope(xp1, xm1, xp2, xm2)
        ay = slope(yp1, ym1, yp2, ym2)
        near = (xp1 + xm1) + (yp1 + ym1)
        far = (xp2 + xm2) + (yp2 + ym2)
        return ax, ay, 4.0 * (near - 3.0 * q) - far

    def finish(c, l, t, change):
        f = c * levels + l
        new = rows_of(src, f, t) + FILTER * change.astype(jnp.float32)
        dst[f, pl.ds(pl.multiple_of(t * SUBS, SUBS), SUBS), :] = new

    for k in range(count):
        t = first + k
        gx, gf = (rows_of(coef, i, t).astype(jnp.bfloat16) for i in range(2))
        hx, hy = [], []
        for l in range(levels):
            ax, ay, smooth = parts(0, l, k)
            hx.append(ax)
            hy.append(ay)
            h, u = get(l, k), get(levels + l, k)
            east = slope(*lon_shifts(u + h * u, halves, lane))
            north = slope(*(north_flux(l, k + d) for d in (1, -1, 2, -2)))
            finish(0, l, t, smooth - (gx * east + gy * north))
        px, py = level_sums(hx), level_sums(hy)
        for l in range(levels):
            u, v = get(levels + l, k), get(2 * levels + l, k)
            ax, ay, smooth = parts(1, l, k)
            finish(1, l, t, smooth - gx * (u * ax + px[l]) - v * (gy * ay - gf))
            ax, ay, smooth = parts(2, l, k)
            finish(2, l, t, smooth - u * (gx * ax + gf) - gy * (v * ay + py[l]))


UNROLL = 4


def member_kernel(levels, halves, blocks, place_ref, own_ref, low_ref, high_ref, lat_ref, lon_ref, coef_ref, *rest):
    outs, (one, two, coef, ready) = rest[:-4], rest[-4:]
    rows = own_ref.shape[2]
    half_rows = rows // halves
    length = half_rows + 2 * MARGIN
    place = place_ref[0]

    for which in range(2):
        for t in range(length):
            coef[which, t * SUBS : (t + 1) * SUBS, :] = jnp.broadcast_to(coef_ref[which, :, t : t + 1], (SUBS, LANES))

    def load(l, carry):
        added = lax.dot_general(
            lat_ref[l], lon_ref[l], (((0,), (0,)), ((), ())),
            precision=lax.Precision.HIGHEST, preferred_element_type=jnp.float32,
        )
        for c in range(3):
            whole = jnp.concatenate(
                [r[c, l].astype(jnp.float32) for r in (low_ref, own_ref, high_ref)], axis=0
            )
            if c == 0:
                whole = (whole + added[: rows + 2 * MARGIN]).astype(jnp.bfloat16).astype(jnp.float32)
            for half in range(halves):
                for b in range(blocks):
                    for t in range(0, length, TILE):
                        at = half * half_rows + t
                        one[c * levels + l, pl.ds(t * SUBS + b * halves + half, TILE, stride=SUBS), :] = whole[
                            at : at + TILE, b * LANES : (b + 1) * LANES
                        ]
        return carry

    lax.fori_loop(0, levels, load, 0)

    src, dst = one, two
    for step in range(STEPS):
        begin = 2 * (step + 1)
        count = length - 2 * begin

        def body(i, carry, src=src, dst=dst, begin=begin):
            step_rows(src, dst, coef, begin + i * UNROLL, UNROLL, halves, levels)
            return carry

        lax.fori_loop(0, count // UNROLL, body, 0)
        if step < STEPS - 1:
            @pl.when((place_ref[1] == 0) | (place_ref[1] == place_ref[2] - 1))
            def _(dst=dst, begin=begin):
                def clear(f, carry):
                    for t in list(range(begin, MARGIN)) + list(range(length - MARGIN, length - begin)):
                        inside = coef_ref[2, :, t : t + 1] > 0.5
                        at = slice(t * SUBS, (t + 1) * SUBS)
                        dst[f, at, :] = jnp.where(inside, dst[f, at, :], 0.0)
                    return carry

                lax.fori_loop(0, 3 * levels, clear, 0)
        src, dst = dst, src

    total = levels * rows
    per = len(outs)
    width = blocks * LANES // per
    for c in range(3):
        for b in range(blocks):
            tiles = []
            for l in range(levels):
                for half in range(halves):
                    for t in range(MARGIN, MARGIN + half_rows, TILE):
                        tiles.append(src[c * levels + l, pl.ds(t * SUBS + b * halves + half, TILE, stride=SUBS), :])
            for j in range(total // LANES):
                square = jnp.concatenate(tiles[j * (LANES // TILE) : (j + 1) * (LANES // TILE)], axis=0)
                turned = square.T.astype(jnp.bfloat16)
                for d in range(LANES // width):
                    ready[b * (LANES // width) + d, c, :, j * LANES : (j + 1) * LANES] = turned[d * width : (d + 1) * width]
    for k in range(per):
        outs[k][...] = ready[place_ref[3 + k]]


def gather_kernel(levels, rows, place_ref, *refs):
    ins, out_ref, held = refs[:-2], refs[-2], refs[-1]
    n = len(ins)
    for k in range(n):
        held[place_ref[3 + k]] = ins[k][...]
    width = ins[0].shape[1]
    for c in range(3):
        for l in range(levels):
            out_ref[c, l] = jnp.concatenate(
                [held[s, c, :, l * rows : (l + 1) * rows] for s in range(n)], axis=1
            )


def shards(analysis, zonal_waves, meridional_waves, amplitude_codes):
    n = lax.axis_size("gx")
    place = lax.axis_index("gx")
    _, levels, rows, lon_total = analysis.shape
    lat_total = rows * n
    blocks = lon_total // LANES
    halves = SUBS // blocks
    half_rows = rows // halves
    length = half_rows + 2 * MARGIN
    width = lon_total // n
    total = levels * rows

    ahead = [(i, i + 1) for i in range(n - 1)]
    back = [(i + 1, i) for i in range(n - 1)]
    low = lax.ppermute(analysis[:, :, rows - MARGIN :], "gx", ahead)
    high = lax.ppermute(analysis[:, :, :MARGIN], "gx", back)

    modes = zonal_waves.shape[1]
    lon_cells = jnp.arange(lon_total, dtype=jnp.int32)
    lon_phase = (lon_cells[None, None, :] * zonal_waves[:, :, None] % lon_total).astype(jnp.float32) * (
        2.0 * math.pi / lon_total
    )
    weights = (AMP_UNIT * amplitude_codes.astype(jnp.float32))[:, :, None]
    lon_table = jnp.concatenate([weights * jnp.cos(lon_phase), -weights * jnp.sin(lon_phase)], axis=1)
    padded = -(-(rows + 2 * MARGIN) // LANES) * LANES
    lat_cells = place * rows - MARGIN + jnp.arange(padded, dtype=jnp.int32)
    inside = (lat_cells >= 0) & (lat_cells < lat_total)
    lat_phase = (lat_cells[None, None, :] * meridional_waves[:, :, None] % lat_total).astype(jnp.float32) * (
        2.0 * math.pi / lat_total
    )
    lat_table = jnp.concatenate([jnp.cos(lat_phase), jnp.sin(lat_phase)], axis=1)
    lat_table = jnp.where(inside[None, None, :], lat_table, 0.0)

    half_of = jnp.arange(SUBS, dtype=jnp.int32) % halves
    cell = place * rows - MARGIN + half_of[:, None] * half_rows + jnp.arange(length, dtype=jnp.int32)[None, :]
    latitude = math.pi / 3.0 * (2.0 * (cell.astype(jnp.float32) + 0.5) / lat_total - 1.0)
    valid = (cell >= 0) & (cell < lat_total)
    factor = (TIME_STEP / 12.0 / FILTER) / jnp.cos(latitude)
    turning = (2.0 * TIME_STEP / FILTER) * jnp.sin(latitude)
    coef = jnp.stack([factor, turning, valid.astype(jnp.float32)])

    order = jnp.arange(n, dtype=jnp.int32) ^ place
    scalars = jnp.concatenate([jnp.stack([place, place, jnp.int32(n)]).astype(jnp.int32), order])

    vmem = pl.BlockSpec(memory_space=pltpu.VMEM)
    smem = pl.BlockSpec(memory_space=pltpu.SMEM)
    piece = jax.ShapeDtypeStruct((3, width, total), jnp.bfloat16)
    sent = pl.pallas_call(
        functools.partial(member_kernel, levels, halves, blocks),
        out_shape=[piece] * n,
        in_specs=[smem] + [vmem] * 6,
        out_specs=[vmem] * n,
        scratch_shapes=[
            pltpu.VMEM((3 * levels, length * SUBS, LANES), jnp.float32),
            pltpu.VMEM((3 * levels, length * SUBS, LANES), jnp.float32),
            pltpu.VMEM((2, length * SUBS, LANES), jnp.float32),
            pltpu.VMEM((n, 3, width, total), jnp.bfloat16),
        ],
        compiler_params=pltpu.CompilerParams(vmem_limit_bytes=56 * 1024 * 1024),
        name="member_steps",
    )(scalars, analysis, low, high, lat_table, lon_table, coef)

    got = [None] * n
    got[0] = sent[0]
    for k in reversed(range(1, n)):
        got[k] = lax.ppermute(sent[k], "gx", [(i, i ^ k) for i in range(n)])
    return pl.pallas_call(
        functools.partial(gather_kernel, levels, rows),
        out_shape=jax.ShapeDtypeStruct((3, levels, width, lat_total), jnp.bfloat16),
        in_specs=[smem] + [vmem] * n,
        out_specs=vmem,
        scratch_shapes=[pltpu.VMEM((n, 3, width, total), jnp.bfloat16)],
        compiler_params=pltpu.CompilerParams(vmem_limit_bytes=48 * 1024 * 1024),
        name="lay_out",
    )(scalars, *got)


def solution(mesh):
    placed = (P(None, None, "gx", None), P("member", None), P("member", None), P("member", None))
    return jax.shard_map(
        shards, mesh=mesh, in_specs=placed, out_specs=P("member", None, "gx", None), check_vma=False
    )
```

```python
import functools
import math

import jax
import jax.numpy as jnp
from jax import lax
from jax.experimental import pallas as pl
from jax.experimental.pallas import tpu as pltpu
from jax.sharding import PartitionSpec as P

NY = 1536
STEPS = 4
TIME_STEP = 0.15
FILTER = 0.03
GRAVITY = 0.5
AMP_UNIT = 0.04
LANES = 128
SUBS = 16
TILE = 8
GROUPS = SUBS // TILE
MARGIN = 2 * STEPS


def lon_shifts(x, halves, lane):
    ahead = pltpu.roll(x, SUBS - halves, 0)
    behind = pltpu.roll(x, halves, 0)
    return (
        pltpu.roll(jnp.where(lane < 1, ahead, x), LANES - 1, 1),
        pltpu.roll(jnp.where(lane >= LANES - 1, behind, x), 1, 1),
        pltpu.roll(jnp.where(lane < 2, ahead, x), LANES - 2, 1),
        pltpu.roll(jnp.where(lane >= LANES - 2, behind, x), 2, 1),
    )


def slope(p1, m1, p2, m2):
    return 8.0 * (p1 - m1) - (p2 - m2)


def level_sums(slopes):
    below = [None] * len(slopes)
    running = None
    for k in reversed(range(len(slopes))):
        running = slopes[k] if running is None else running + slopes[k]
        below[k] = running
    return [(0.5 * GRAVITY) * (running + b) for b in below]


def rows_of(ref, f, t):
    at = pl.ds(pl.multiple_of(t * TILE, TILE), TILE)
    return jnp.concatenate([ref[f, g, at, :] for g in range(GROUPS)], axis=0)


def step_rows(src, dst, coef, first, count, halves, levels):
    lane = lax.broadcasted_iota(jnp.int32, (SUBS, LANES), 1)
    gy = TIME_STEP / 12.0 / FILTER
    loaded = {}

    def get(f, k):
        if (f, k) not in loaded:
            loaded[f, k] = rows_of(src, f, first + k).astype(jnp.bfloat16)
        return loaded[f, k]

    flux = {}

    def north_flux(l, k):
        if (l, k) not in flux:
            v = get(2 * levels + l, k)
            flux[l, k] = v + get(l, k) * v
        return flux[l, k]

    def parts(c, l, k):
        q = get(c * levels + l, k)
        xp1, xm1, xp2, xm2 = lon_shifts(q, halves, lane)
        yp1, ym1, yp2, ym2 = (get(c * levels + l, k + d) for d in (1, -1, 2, -2))
        ax = slope(xp1, xm1, xp2, xm2)
        ay = slope(yp1, ym1, yp2, ym2)
        near = (xp1 + xm1) + (yp1 + ym1)
        far = (xp2 + xm2) + (yp2 + ym2)
        return ax, ay, 4.0 * near - far

    def finish(c, l, t, change):
        f = c * levels + l
        new = (1.0 - 12.0 * FILTER) * rows_of(src, f, t) + FILTER * change.astype(jnp.float32)
        at = pl.ds(pl.multiple_of(t * TILE, TILE), TILE)
        for g in range(GROUPS):
            dst[f, g, at, :] = new[g * TILE : (g + 1) * TILE]

    for k in range(count):
        t = first + k
        gx, gf = (rows_of(coef, i, t).astype(jnp.bfloat16) for i in range(2))
        hx, hy = [], []
        for l in range(levels):
            ax, ay, smooth = parts(0, l, k)
            hx.append(ax)
            hy.append(ay)
            h, u = get(l, k), get(levels + l, k)
            east = slope(*lon_shifts(u + h * u, halves, lane))
            north = slope(*(north_flux(l, k + d) for d in (1, -1, 2, -2)))
            finish(0, l, t, smooth - (gx * east + gy * north))
        px, py = level_sums(hx), level_sums(hy)
        for l in range(levels):
            u, v = get(levels + l, k), get(2 * levels + l, k)
            ax, ay, smooth = parts(1, l, k)
            finish(1, l, t, smooth - (gx * (u * ax + px[l]) + v * (gy * ay - gf)))
            ax, ay, smooth = parts(2, l, k)
            finish(2, l, t, smooth - (u * (gx * ax + gf) + gy * (v * ay + py[l])))


UNROLL = 4


def member_kernel(levels, halves, blocks, place_ref, own_ref, low_ref, high_ref, lat_ref, lon_ref, coef_ref, *rest):
    outs, (one, two, coef, ready) = rest[:-4], rest[-4:]
    rows = own_ref.shape[2]
    half_rows = rows // halves
    length = half_rows + 2 * MARGIN
    place = place_ref[0]

    for which in range(2):
        for t in range(length):
            for g in range(GROUPS):
                coef[which, g, t * TILE : (t + 1) * TILE, :] = jnp.broadcast_to(
                    coef_ref[which, :TILE, t : t + 1], (TILE, LANES)
                )

    def load(l, carry):
        added = lax.dot_general(
            lat_ref[l], lon_ref[l], (((0,), (0,)), ((), ())),
            precision=lax.Precision.HIGHEST, preferred_element_type=jnp.float32,
        )
        for c in range(3):
            whole = jnp.concatenate(
                [r[c, l].astype(jnp.float32) for r in (low_ref, own_ref, high_ref)], axis=0
            )
            if c == 0:
                whole = (whole + added[: rows + 2 * MARGIN]).astype(jnp.bfloat16).astype(jnp.float32)
            for half in range(halves):
                for b in range(blocks):
                    for t in range(0, length, TILE):
                        at = half * half_rows + t
                        spot = b * halves + half
                        one[c * levels + l, spot // TILE, pl.ds(t * TILE + spot % TILE, TILE, stride=TILE), :] = whole[
                            at : at + TILE, b * LANES : (b + 1) * LANES
                        ]
        return carry

    lax.fori_loop(0, levels, load, 0)

    src, dst = one, two
    for step in range(STEPS):
        begin = 2 * (step + 1)
        count = length - 2 * begin

        def body(i, carry, src=src, dst=dst, begin=begin):
            step_rows(src, dst, coef, begin + i * UNROLL, UNROLL, halves, levels)
            return carry

        lax.fori_loop(0, count // UNROLL, body, 0)
        if step < STEPS - 1:
            @pl.when((place_ref[1] == 0) | (place_ref[1] == place_ref[2] - 1))
            def _(dst=dst, begin=begin):
                def clear(f, carry):
                    for t in list(range(begin, MARGIN)) + list(range(length - MARGIN, length - begin)):
                        inside = coef_ref[2, :TILE, t : t + 1] > 0.5
                        at = slice(t * TILE, (t + 1) * TILE)
                        for g in range(GROUPS):
                            dst[f, g, at, :] = jnp.where(inside, dst[f, g, at, :], 0.0)
                    return carry

                lax.fori_loop(0, 3 * levels, clear, 0)
        src, dst = dst, src

    total = levels * rows
    per = len(outs)
    width = blocks * LANES // per
    for c in range(3):
        for b in range(blocks):
            tiles = []
            for l in range(levels):
                for half in range(halves):
                    for t in range(MARGIN, MARGIN + half_rows, TILE):
                        spot = b * halves + half
                        at = pl.ds(t * TILE + spot % TILE, TILE, stride=TILE)
                        tiles.append(src[c * levels + l, spot // TILE, at, :])
            for j in range(total // LANES):
                square = jnp.concatenate(tiles[j * (LANES // TILE) : (j + 1) * (LANES // TILE)], axis=0)
                turned = square.T.astype(jnp.bfloat16)
                for d in range(LANES // width):
                    ready[b * (LANES // width) + d, c, :, j * LANES : (j + 1) * LANES] = turned[d * width : (d + 1) * width]
    for k in range(per):
        outs[k][...] = ready[place_ref[3 + k]]


def gather_kernel(levels, rows, place_ref, *refs):
    ins, out_ref, held = refs[:-2], refs[-2], refs[-1]
    n = len(ins)
    for k in range(n):
        held[place_ref[3 + k]] = ins[k][...]
    width = ins[0].shape[1]
    for c in range(3):
        for l in range(levels):
            out_ref[c, l] = jnp.concatenate(
                [held[s, c, :, l * rows : (l + 1) * rows] for s in range(n)], axis=1
            )


def shards(analysis, zonal_waves, meridional_waves, amplitude_codes):
    n = lax.axis_size("gx")
    place = lax.axis_index("gx")
    _, levels, rows, lon_total = analysis.shape
    lat_total = rows * n
    blocks = lon_total // LANES
    halves = SUBS // blocks
    half_rows = rows // halves
    length = half_rows + 2 * MARGIN
    width = lon_total // n
    total = levels * rows

    ahead = [(i, i + 1) for i in range(n - 1)]
    back = [(i + 1, i) for i in range(n - 1)]
    low = lax.ppermute(analysis[:, :, rows - MARGIN :], "gx", ahead)
    high = lax.ppermute(analysis[:, :, :MARGIN], "gx", back)

    modes = zonal_waves.shape[1]
    lon_cells = jnp.arange(lon_total, dtype=jnp.int32)
    lon_phase = (lon_cells[None, None, :] * zonal_waves[:, :, None] % lon_total).astype(jnp.float32) * (
        2.0 * math.pi / lon_total
    )
    weights = (AMP_UNIT * amplitude_codes.astype(jnp.float32))[:, :, None]
    lon_table = jnp.concatenate([weights * jnp.cos(lon_phase), -weights * jnp.sin(lon_phase)], axis=1)
    padded = -(-(rows + 2 * MARGIN) // LANES) * LANES
    lat_cells = place * rows - MARGIN + jnp.arange(padded, dtype=jnp.int32)
    inside = (lat_cells >= 0) & (lat_cells < lat_total)
    lat_phase = (lat_cells[None, None, :] * meridional_waves[:, :, None] % lat_total).astype(jnp.float32) * (
        2.0 * math.pi / lat_total
    )
    lat_table = jnp.concatenate([jnp.cos(lat_phase), jnp.sin(lat_phase)], axis=1)
    lat_table = jnp.where(inside[None, None, :], lat_table, 0.0)

    half_of = jnp.arange(SUBS, dtype=jnp.int32) % halves
    cell = place * rows - MARGIN + half_of[:, None] * half_rows + jnp.arange(length, dtype=jnp.int32)[None, :]
    latitude = math.pi / 3.0 * (2.0 * (cell.astype(jnp.float32) + 0.5) / lat_total - 1.0)
    valid = (cell >= 0) & (cell < lat_total)
    factor = (TIME_STEP / 12.0 / FILTER) / jnp.cos(latitude)
    turning = (2.0 * TIME_STEP / FILTER) * jnp.sin(latitude)
    coef = jnp.stack([factor, turning, valid.astype(jnp.float32)])

    order = [0]
    reach = n
    while reach > 1:
        order += range(reach // 2, reach)
        reach //= 2
    partners = jnp.stack([place ^ k for k in order])
    scalars = jnp.concatenate([jnp.stack([place, place, jnp.int32(n)]), partners]).astype(jnp.int32)

    vmem = pl.BlockSpec(memory_space=pltpu.VMEM)
    smem = pl.BlockSpec(memory_space=pltpu.SMEM)
    piece = jax.ShapeDtypeStruct((3, width, total), jnp.bfloat16)
    sent = pl.pallas_call(
        functools.partial(member_kernel, levels, halves, blocks),
        out_shape=[piece] * n,
        in_specs=[smem] + [vmem] * 6,
        out_specs=[vmem] * n,
        scratch_shapes=[
            pltpu.VMEM((3 * levels, GROUPS, length * TILE, LANES), jnp.float32),
            pltpu.VMEM((3 * levels, GROUPS, length * TILE, LANES), jnp.float32),
            pltpu.VMEM((2, GROUPS, length * TILE, LANES), jnp.float32),
            pltpu.VMEM((n, 3, width, total), jnp.bfloat16),
        ],
        compiler_params=pltpu.CompilerParams(vmem_limit_bytes=24 * 1024 * 1024),
        name="member_steps",
    )(scalars, analysis, low, high, lat_table, lon_table, coef)

    got = [sent[0]]
    for piece_of, k in list(zip(sent, order))[1:]:
        got.append(lax.ppermute(piece_of, "gx", [(i, i ^ k) for i in range(n)]))
    return pl.pallas_call(
        functools.partial(gather_kernel, levels, rows),
        out_shape=jax.ShapeDtypeStruct((3, levels, width, lat_total), jnp.bfloat16),
        in_specs=[smem] + [vmem] * n,
        out_specs=vmem,
        scratch_shapes=[pltpu.VMEM((n, 3, width, total), jnp.bfloat16)],
        compiler_params=pltpu.CompilerParams(vmem_limit_bytes=12 * 1024 * 1024),
        name="lay_out",
    )(scalars, *got)


def solution(mesh):
    placed = (P(None, None, "gx", None), P("member", None), P("member", None), P("member", None))
    return jax.shard_map(
        shards, mesh=mesh, in_specs=placed, out_specs=P("member", None, "gx", None), check_vma=False
    )
```

```python
import functools
import math

import jax
import jax.numpy as jnp
import numpy as np
from jax import lax
from jax.experimental import pallas as pl
from jax.experimental.pallas import tpu as pltpu
from jax.sharding import PartitionSpec as P

NY = 1536
STEPS = 4
TIME_STEP = 0.15
FILTER = 0.03
GRAVITY = 0.5
AMP_UNIT = 0.04
LANES = 128
SUBS = 16
TILE = 8
GROUPS = SUBS // TILE
MARGIN = 2 * STEPS


def lon_operators():
    table = np.zeros((2 * LANES, 2 * LANES), np.float32)
    for lane in range(LANES):
        for reach, slope_by, smooth_by in ((1, 8.0, 4.0), (-1, -8.0, 4.0), (2, -1.0, -1.0), (-2, 1.0, -1.0)):
            at = lane + reach
            row = at if 0 <= at < LANES else LANES + at % LANES
            table[row, lane] = slope_by
            table[row, LANES + lane] = smooth_by
    return jnp.asarray(table, jnp.bfloat16)


def with_ends(x, halves, lane):
    ahead = pltpu.roll(x, SUBS - halves, 0)
    behind = pltpu.roll(x, halves, 0)
    return jnp.concatenate([x, jnp.where(lane < 2, ahead, behind)], axis=1)


def slope(p1, m1, p2, m2):
    return 8.0 * (p1 - m1) - (p2 - m2)


def level_sums(slopes):
    below = [None] * len(slopes)
    running = None
    for k in reversed(range(len(slopes))):
        running = slopes[k] if running is None else running + slopes[k]
        below[k] = running
    return [(0.5 * GRAVITY) * (running + b) for b in below]


def rows_of(ref, f, t):
    at = pl.ds(pl.multiple_of(t * TILE, TILE), TILE)
    return jnp.concatenate([ref[f, g, at, :] for g in range(GROUPS)], axis=0)


def step_rows(src, dst, coef, table, first, count, halves, levels):
    lane = lax.broadcasted_iota(jnp.int32, (SUBS, LANES), 1)
    gy = TIME_STEP / 12.0 / FILTER
    loaded = {}

    def get(f, k):
        if (f, k) not in loaded:
            loaded[f, k] = rows_of(src, f, first + k).astype(jnp.bfloat16)
        return loaded[f, k]

    flux = {}

    def north_flux(l, k):
        if (l, k) not in flux:
            v = get(2 * levels + l, k)
            flux[l, k] = v + get(l, k) * v
        return flux[l, k]

    def lon_parts(k):
        pieces = [with_ends(get(f, k), halves, lane) for f in range(3 * levels)]
        both = jnp.dot(jnp.concatenate(pieces, axis=0), table[...], preferred_element_type=jnp.float32)
        fluxes = []
        for l in range(levels):
            u = get(levels + l, k)
            fluxes.append(with_ends(u + get(l, k) * u, halves, lane))
        east = jnp.dot(jnp.concatenate(fluxes, axis=0), table[:, :LANES], preferred_element_type=jnp.float32)
        return both, east

    for k in range(count):
        t = first + k
        both, east_of = lon_parts(k)

        def parts(c, l):
            f = c * levels + l
            at = slice(f * SUBS, (f + 1) * SUBS)
            yp1, ym1, yp2, ym2 = (get(f, k + d) for d in (1, -1, 2, -2))
            ax = both[at, :LANES].astype(jnp.bfloat16)
            return ax, slope(yp1, ym1, yp2, ym2), 4.0 * (yp1 + ym1) - (yp2 + ym2), both[at, LANES:]

        def finish(c, l, smooth, change):
            f = c * levels + l
            change = smooth + change.astype(jnp.float32)
            new = (1.0 - 12.0 * FILTER) * rows_of(src, f, t) + FILTER * change
            at = pl.ds(pl.multiple_of(t * TILE, TILE), TILE)
            for g in range(GROUPS):
                dst[f, g, at, :] = new[g * TILE : (g + 1) * TILE]

        gx, gf = (rows_of(coef, i, t).astype(jnp.bfloat16) for i in range(2))
        hx, hy = [], []
        for l in range(levels):
            ax, ay, sy, sx = parts(0, l)
            hx.append(ax)
            hy.append(ay)
            east = east_of[l * SUBS : (l + 1) * SUBS].astype(jnp.bfloat16)
            north = slope(*(north_flux(l, k + d) for d in (1, -1, 2, -2)))
            finish(0, l, sx, sy - (gx * east + gy * north))
        px, py = level_sums(hx), level_sums(hy)
        for l in range(levels):
            u, v = get(levels + l, k), get(2 * levels + l, k)
            ax, ay, sy, sx = parts(1, l)
            finish(1, l, sx, sy - (gx * (u * ax + px[l]) + v * (gy * ay - gf)))
            ax, ay, sy, sx = parts(2, l)
            finish(2, l, sx, sy - (u * (gx * ax + gf) + gy * (v * ay + py[l])))


UNROLL = 4


def member_kernel(levels, halves, blocks, place_ref, own_ref, low_ref, high_ref, lat_ref, lon_ref, coef_ref, table, *rest):
    outs, (one, two, coef, ready) = rest[:-4], rest[-4:]
    rows = own_ref.shape[2]
    half_rows = rows // halves
    length = half_rows + 2 * MARGIN
    place = place_ref[0]

    for which in range(3):
        for t in range(length):
            for g in range(GROUPS):
                coef[which, g, t * TILE : (t + 1) * TILE, :] = jnp.broadcast_to(
                    coef_ref[which, :TILE, t : t + 1], (TILE, LANES)
                )

    def load(l, carry):
        added = lax.dot_general(
            lat_ref[l], lon_ref[l], (((0,), (0,)), ((), ())),
            precision=lax.Precision.HIGHEST, preferred_element_type=jnp.float32,
        )
        for c in range(3):
            whole = jnp.concatenate(
                [r[c, l].astype(jnp.float32) for r in (low_ref, own_ref, high_ref)], axis=0
            )
            if c == 0:
                whole = (whole + added[: rows + 2 * MARGIN]).astype(jnp.bfloat16).astype(jnp.float32)
            for half in range(halves):
                for b in range(blocks):
                    for t in range(0, length, TILE):
                        at = half * half_rows + t
                        spot = b * halves + half
                        one[c * levels + l, spot // TILE, pl.ds(t * TILE + spot % TILE, TILE, stride=TILE), :] = whole[
                            at : at + TILE, b * LANES : (b + 1) * LANES
                        ]
        return carry

    lax.fori_loop(0, levels, load, 0)

    src, dst = one, two
    for step in range(STEPS):
        begin = 2 * (step + 1)
        count = length - 2 * begin

        def body(i, carry, src=src, dst=dst, begin=begin):
            step_rows(src, dst, coef, table, begin + i * UNROLL, UNROLL, halves, levels)
            return carry

        lax.fori_loop(0, count // UNROLL, body, 0)
        if step < STEPS - 1:
            @pl.when((place_ref[1] == 0) | (place_ref[1] == place_ref[2] - 1))
            def _(dst=dst, begin=begin):
                def clear(f, carry):
                    for t in list(range(begin, MARGIN)) + list(range(length - MARGIN, length - begin)):
                        at = slice(t * TILE, (t + 1) * TILE)
                        for g in range(GROUPS):
                            dst[f, g, at, :] = jnp.where(coef[2, g, at, :] > 0.5, dst[f, g, at, :], 0.0)
                    return carry

                lax.fori_loop(0, 3 * levels, clear, 0)
        src, dst = dst, src

    total = levels * rows
    per = len(outs)
    width = blocks * LANES // per
    for c in range(3):
        for b in range(blocks):
            tiles = []
            for l in range(levels):
                for half in range(halves):
                    for t in range(MARGIN, MARGIN + half_rows, TILE):
                        spot = b * halves + half
                        at = pl.ds(t * TILE + spot % TILE, TILE, stride=TILE)
                        tiles.append(src[c * levels + l, spot // TILE, at, :])
            for j in range(total // LANES):
                square = jnp.concatenate(tiles[j * (LANES // TILE) : (j + 1) * (LANES // TILE)], axis=0)
                turned = square.T.astype(jnp.bfloat16)
                for d in range(LANES // width):
                    ready[b * (LANES // width) + d, c, :, j * LANES : (j + 1) * LANES] = turned[d * width : (d + 1) * width]
    for k in range(per):
        outs[k][...] = ready[place_ref[3 + k]]


def gather_kernel(levels, rows, place_ref, *refs):
    ins, out_ref, held = refs[:-2], refs[-2], refs[-1]
    n = len(ins)
    for k in range(n):
        held[place_ref[3 + k]] = ins[k][...]
    width = ins[0].shape[1]
    for c in range(3):
        for l in range(levels):
            out_ref[c, l] = jnp.concatenate(
                [held[s, c, :, l * rows : (l + 1) * rows] for s in range(n)], axis=1
            )


def shards(analysis, zonal_waves, meridional_waves, amplitude_codes):
    n = lax.axis_size("gx")
    place = lax.axis_index("gx")
    _, levels, rows, lon_total = analysis.shape
    lat_total = rows * n
    blocks = lon_total // LANES
    halves = SUBS // blocks
    half_rows = rows // halves
    length = half_rows + 2 * MARGIN
    width = lon_total // n
    total = levels * rows

    ahead = [(i, i + 1) for i in range(n - 1)]
    back = [(i + 1, i) for i in range(n - 1)]
    low = lax.ppermute(analysis[:, :, rows - MARGIN :], "gx", ahead)
    high = lax.ppermute(analysis[:, :, :MARGIN], "gx", back)

    modes = zonal_waves.shape[1]
    lon_cells = jnp.arange(lon_total, dtype=jnp.int32)
    lon_phase = (lon_cells[None, None, :] * zonal_waves[:, :, None] % lon_total).astype(jnp.float32) * (
        2.0 * math.pi / lon_total
    )
    weights = (AMP_UNIT * amplitude_codes.astype(jnp.float32))[:, :, None]
    lon_table = jnp.concatenate([weights * jnp.cos(lon_phase), -weights * jnp.sin(lon_phase)], axis=1)
    padded = -(-(rows + 2 * MARGIN) // LANES) * LANES
    lat_cells = place * rows - MARGIN + jnp.arange(padded, dtype=jnp.int32)
    inside = (lat_cells >= 0) & (lat_cells < lat_total)
    lat_phase = (lat_cells[None, None, :] * meridional_waves[:, :, None] % lat_total).astype(jnp.float32) * (
        2.0 * math.pi / lat_total
    )
    lat_table = jnp.concatenate([jnp.cos(lat_phase), jnp.sin(lat_phase)], axis=1)
    lat_table = jnp.where(inside[None, None, :], lat_table, 0.0)

    half_of = jnp.arange(SUBS, dtype=jnp.int32) % halves
    cell = place * rows - MARGIN + half_of[:, None] * half_rows + jnp.arange(length, dtype=jnp.int32)[None, :]
    latitude = math.pi / 3.0 * (2.0 * (cell.astype(jnp.float32) + 0.5) / lat_total - 1.0)
    valid = (cell >= 0) & (cell < lat_total)
    factor = (TIME_STEP / 12.0 / FILTER) / jnp.cos(latitude)
    turning = (2.0 * TIME_STEP / FILTER) * jnp.sin(latitude)
    coef = jnp.stack([factor, turning, valid.astype(jnp.float32)])

    order = [0]
    reach = n
    while reach > 1:
        order += range(reach // 2, reach)
        reach //= 2
    partners = jnp.stack([place ^ k for k in order])
    scalars = jnp.concatenate([jnp.stack([place, place, jnp.int32(n)]), partners]).astype(jnp.int32)

    vmem = pl.BlockSpec(memory_space=pltpu.VMEM)
    smem = pl.BlockSpec(memory_space=pltpu.SMEM)
    piece = jax.ShapeDtypeStruct((3, width, total), jnp.bfloat16)
    sent = pl.pallas_call(
        functools.partial(member_kernel, levels, halves, blocks),
        out_shape=[piece] * n,
        in_specs=[smem] + [vmem] * 7,
        out_specs=[vmem] * n,
        scratch_shapes=[
            pltpu.VMEM((3 * levels, GROUPS, length * TILE, LANES), jnp.float32),
            pltpu.VMEM((3 * levels, GROUPS, length * TILE, LANES), jnp.float32),
            pltpu.VMEM((3, GROUPS, length * TILE, LANES), jnp.float32),
            pltpu.VMEM((n, 3, width, total), jnp.bfloat16),
        ],
        compiler_params=pltpu.CompilerParams(vmem_limit_bytes=24 * 1024 * 1024),
        name="member_steps",
    )(scalars, analysis, low, high, lat_table, lon_table, coef, lon_operators())

    got = [sent[0]]
    for piece_of, k in list(zip(sent, order))[1:]:
        got.append(lax.ppermute(piece_of, "gx", [(i, i ^ k) for i in range(n)]))
    return pl.pallas_call(
        functools.partial(gather_kernel, levels, rows),
        out_shape=jax.ShapeDtypeStruct((3, levels, width, lat_total), jnp.bfloat16),
        in_specs=[smem] + [vmem] * n,
        out_specs=vmem,
        scratch_shapes=[pltpu.VMEM((n, 3, width, total), jnp.bfloat16)],
        compiler_params=pltpu.CompilerParams(vmem_limit_bytes=12 * 1024 * 1024),
        name="lay_out",
    )(scalars, *got)


def solution(mesh):
    placed = (P(None, None, "gx", None), P("member", None), P("member", None), P("member", None))
    return jax.shard_map(
        shards, mesh=mesh, in_specs=placed, out_specs=P("member", None, "gx", None), check_vma=False
    )
```

```python
import functools
import math

import jax
import jax.numpy as jnp
from jax import lax
from jax.experimental import pallas as pl
from jax.experimental.pallas import tpu as pltpu
from jax.sharding import PartitionSpec as P

NY = 1536
STEPS = 4
TIME_STEP = 0.15
FILTER = 0.03
GRAVITY = 0.5
AMP_UNIT = 0.04
LANES = 128
SUBS = 16
TILE = 8
GROUPS = SUBS // TILE
MARGIN = 2 * STEPS


def lon_operators():
    shape = (2 * LANES, 2 * LANES)
    row = lax.broadcasted_iota(jnp.int32, shape, 0)
    column = lax.broadcasted_iota(jnp.int32, shape, 1)
    at = jnp.where(row < LANES + 2, row, jnp.where(row >= 2 * LANES - 2, row - 2 * LANES, -LANES))
    reach = at - jnp.where(column < LANES, column, column - LANES)
    size = jnp.abs(reach)
    slopes = jnp.where(size == 1, 8.0, jnp.where(size == 2, -1.0, 0.0)) * jnp.where(reach > 0, 1.0, -1.0)
    smooths = jnp.where(size == 1, 4.0, jnp.where(size == 2, -1.0, 0.0))
    return jnp.where(column < LANES, slopes, smooths).astype(jnp.bfloat16)


def with_ends(x, halves, lane):
    ahead = pltpu.roll(x, SUBS - halves, 0)
    behind = pltpu.roll(x, halves, 0)
    return jnp.concatenate([x, jnp.where(lane < 2, ahead, behind)], axis=1)


def slope(p1, m1, p2, m2):
    return 8.0 * (p1 - m1) - (p2 - m2)


def level_sums(slopes):
    below = [None] * len(slopes)
    running = None
    for k in reversed(range(len(slopes))):
        running = slopes[k] if running is None else running + slopes[k]
        below[k] = running
    return [(0.5 * GRAVITY) * (running + b) for b in below]


def rows_of(ref, f, t):
    at = pl.ds(pl.multiple_of(t * TILE, TILE), TILE)
    return jnp.concatenate([ref[f, g, at, :] for g in range(GROUPS)], axis=0)


def step_rows(src, dst, coef, table, first, count, halves, levels):
    lane = lax.broadcasted_iota(jnp.int32, (SUBS, LANES), 1)
    gy = TIME_STEP / 12.0 / FILTER
    loaded = {}

    def get(f, k):
        if (f, k) not in loaded:
            loaded[f, k] = rows_of(src, f, first + k).astype(jnp.bfloat16)
        return loaded[f, k]

    flux = {}

    def north_flux(l, k):
        if (l, k) not in flux:
            v = get(2 * levels + l, k)
            flux[l, k] = v + get(l, k) * v
        return flux[l, k]

    def lon_parts(k):
        pieces = [with_ends(get(f, k), halves, lane) for f in range(3 * levels)]
        both = jnp.dot(jnp.concatenate(pieces, axis=0), table[...], preferred_element_type=jnp.float32)
        fluxes = []
        for l in range(levels):
            u = get(levels + l, k)
            fluxes.append(with_ends(u + get(l, k) * u, halves, lane))
        east = jnp.dot(jnp.concatenate(fluxes, axis=0), table[:, :LANES], preferred_element_type=jnp.float32)
        return both, east

    for k in range(count):
        t = first + k
        both, east_of = lon_parts(k)

        def parts(c, l):
            f = c * levels + l
            at = slice(f * SUBS, (f + 1) * SUBS)
            yp1, ym1, yp2, ym2 = (get(f, k + d) for d in (1, -1, 2, -2))
            ax = both[at, :LANES].astype(jnp.bfloat16)
            return ax, slope(yp1, ym1, yp2, ym2), 4.0 * (yp1 + ym1) - (yp2 + ym2), both[at, LANES:]

        def finish(c, l, smooth, change):
            f = c * levels + l
            change = smooth + change.astype(jnp.float32)
            new = (1.0 - 12.0 * FILTER) * rows_of(src, f, t) + FILTER * change
            at = pl.ds(pl.multiple_of(t * TILE, TILE), TILE)
            for g in range(GROUPS):
                dst[f, g, at, :] = new[g * TILE : (g + 1) * TILE]

        gx, gf = (rows_of(coef, i, t).astype(jnp.bfloat16) for i in range(2))
        hx, hy = [], []
        for l in range(levels):
            ax, ay, sy, sx = parts(0, l)
            hx.append(ax)
            hy.append(ay)
            east = east_of[l * SUBS : (l + 1) * SUBS].astype(jnp.bfloat16)
            north = slope(*(north_flux(l, k + d) for d in (1, -1, 2, -2)))
            finish(0, l, sx, sy - (gx * east + gy * north))
        px, py = level_sums(hx), level_sums(hy)
        for l in range(levels):
            u, v = get(levels + l, k), get(2 * levels + l, k)
            ax, ay, sy, sx = parts(1, l)
            finish(1, l, sx, sy - (gx * (u * ax + px[l]) + v * (gy * ay - gf)))
            ax, ay, sy, sx = parts(2, l)
            finish(2, l, sx, sy - (u * (gx * ax + gf) + gy * (v * ay + py[l])))


LARGEST_GROUP = 14


def group_of(count):
    return max(k for k in range(1, LARGEST_GROUP + 1) if count % k == 0)


def as_column(row):
    count = row.shape[1]
    square = jnp.broadcast_to(row, (count, count))
    here = lax.broadcasted_iota(jnp.int32, (count, count), 0) == lax.broadcasted_iota(jnp.int32, (count, count), 1)
    return jnp.sum(jnp.where(here, square, 0.0), axis=1, keepdims=True)


def phases(wave, cells, period):
    product = wave * cells
    left = product - jnp.floor(product * (1.0 / period)) * period
    left = jnp.where(left < 0.0, left + period, left)
    left = jnp.where(left >= period, left - period, left)
    return left * (2.0 * math.pi / period)


def put_rows(state, f, t, part, values, parts):
    for b in range(values.shape[1] // LANES):
        spot = b * parts + part
        at = pl.ds(t * TILE + spot % TILE, TILE, stride=TILE)
        state[f, spot // TILE, at, :] = values[:, b * LANES : (b + 1) * LANES]


def prepare_kernel(
    lat_total, halves, place_ref, analysis_ref, zonal_hbm, meridional_hbm, code_hbm,
    state, added_ref, coef, table,
    own_ref, zonal_ref, meridional_ref, code_ref, lon_ref, lat_ref, sems,
):
    copies = [
        pltpu.make_async_copy(source, target, sems.at[i])
        for i, (source, target) in enumerate(
            (
                (zonal_hbm, zonal_ref),
                (meridional_hbm, meridional_ref),
                (code_hbm, code_ref),
                (analysis_ref, own_ref),
            )
        )
    ]
    for copy in copies:
        copy.start()
    levels, modes = zonal_ref.shape
    rows = own_ref.shape[2]
    half_rows = rows // halves
    length = half_rows + 2 * MARGIN
    lon_total, padded = lon_ref.shape[2], lat_ref.shape[2]
    start = place_ref[1] * rows - MARGIN

    table[...] = lon_operators()
    part = lax.broadcasted_iota(jnp.int32, (SUBS, LANES), 0) % halves
    row = start + part * half_rows + lax.broadcasted_iota(jnp.int32, (SUBS, LANES), 1)
    latitude = math.pi / 3.0 * (2.0 * (row.astype(jnp.float32) + 0.5) / lat_total - 1.0)
    factors = (
        (TIME_STEP / 12.0 / FILTER) / jnp.cos(latitude),
        (2.0 * TIME_STEP / FILTER) * jnp.sin(latitude),
        ((row >= 0) & (row < lat_total)).astype(jnp.float32),
    )
    for which in range(3):
        for t in range(length):
            tile = jnp.broadcast_to(factors[which][:TILE, t : t + 1], (TILE, LANES))
            for g in range(GROUPS):
                coef[which, g, t * TILE : (t + 1) * TILE, :] = tile

    lon_cells = lax.broadcasted_iota(jnp.int32, (modes, lon_total), 1).astype(jnp.float32)
    cell = lax.broadcasted_iota(jnp.int32, (modes, padded), 1) + start
    inside = (cell >= 0) & (cell < lat_total)
    lat_cells = jnp.where(inside, cell, 0).astype(jnp.float32)
    for copy in copies[:3]:
        copy.wait()
    for l in range(levels):
        zonal, meridional, code = (
            as_column(r[l : l + 1, :].astype(jnp.float32)) for r in (zonal_ref, meridional_ref, code_ref)
        )
        phase = phases(zonal, lon_cells, lon_total)
        weight = AMP_UNIT * code
        lon_ref[l, :modes, :] = weight * jnp.cos(phase)
        lon_ref[l, modes:, :] = -weight * jnp.sin(phase)
        phase = phases(meridional, lat_cells, lat_total)
        lat_ref[l, :modes, :] = jnp.where(inside, jnp.cos(phase), 0.0)
        lat_ref[l, modes:, :] = jnp.where(inside, jnp.sin(phase), 0.0)

    copies[3].wait()

    def load(l, carry):
        added = lax.dot_general(
            lat_ref[l], lon_ref[l], (((0,), (0,)), ((), ())),
            precision=lax.Precision.HIGHEST, preferred_element_type=jnp.float32,
        )
        added_ref[l, :MARGIN, :] = added[:MARGIN]
        added_ref[l, MARGIN:, :] = added[rows + MARGIN : rows + 2 * MARGIN]
        for c in range(3):
            own = own_ref[c, l].astype(jnp.float32)
            if c == 0:
                own = (own + added[MARGIN : rows + MARGIN]).astype(jnp.bfloat16).astype(jnp.float32)
            for half in range(halves):
                for t in range(0, length, TILE):
                    at = half * half_rows + t - MARGIN
                    if 0 <= at < rows:
                        put_rows(state, c * levels + l, t, half, own[at : at + TILE], halves)
        return carry

    lax.fori_loop(0, levels, load, 0)


def member_kernel(levels, halves, blocks, rows, place_ref, inner_ref, outer_ref, added_ref, coef, table, _, *rest):
    outs, one, (two, ready) = rest[:-3], rest[-3], rest[-2:]
    half_rows = rows // halves
    length = half_rows + 2 * MARGIN
    odd = place_ref[0] == 1

    def load(l, carry):
        for c in range(3):
            inner, outer = (r[c, l].astype(jnp.float32) for r in (inner_ref, outer_ref))
            low, high = jnp.where(odd, inner, outer), jnp.where(odd, outer, inner)
            if c == 0:
                low = (low + added_ref[l, :MARGIN, :]).astype(jnp.bfloat16).astype(jnp.float32)
                high = (high + added_ref[l, MARGIN:, :]).astype(jnp.bfloat16).astype(jnp.float32)
            put_rows(one, c * levels + l, 0, 0, low, halves)
            put_rows(one, c * levels + l, length - MARGIN, halves - 1, high, halves)
        return carry

    lax.fori_loop(0, levels, load, 0)

    src, dst = one, two
    for step in range(STEPS):
        begin = 2 * (step + 1)
        count = length - 2 * begin

        group = group_of(count)

        def body(i, carry, src=src, dst=dst, begin=begin, group=group):
            step_rows(src, dst, coef, table, begin + i * group, group, halves, levels)
            return carry

        lax.fori_loop(0, count // group, body, 0)
        if step < STEPS - 1:
            @pl.when((place_ref[1] == 0) | (place_ref[1] == place_ref[2] - 1))
            def _(dst=dst, begin=begin):
                def clear(f, carry):
                    for t in list(range(begin, MARGIN)) + list(range(length - MARGIN, length - begin)):
                        at = slice(t * TILE, (t + 1) * TILE)
                        for g in range(GROUPS):
                            dst[f, g, at, :] = jnp.where(coef[2, g, at, :] > 0.5, dst[f, g, at, :], 0.0)
                    return carry

                lax.fori_loop(0, 3 * levels, clear, 0)
        src, dst = dst, src

    total = levels * rows
    per = len(outs)
    width = blocks * LANES // per
    for c in range(3):
        for b in range(blocks):
            tiles = []
            for l in range(levels):
                for half in range(halves):
                    for t in range(MARGIN, MARGIN + half_rows, TILE):
                        spot = b * halves + half
                        at = pl.ds(t * TILE + spot % TILE, TILE, stride=TILE)
                        tiles.append(src[c * levels + l, spot // TILE, at, :])
            for j in range(total // LANES):
                square = jnp.concatenate(tiles[j * (LANES // TILE) : (j + 1) * (LANES // TILE)], axis=0)
                turned = square.T.astype(jnp.bfloat16)
                for d in range(LANES // width):
                    ready[b * (LANES // width) + d, c, :, j * LANES : (j + 1) * LANES] = turned[d * width : (d + 1) * width]
    for k in range(per):
        outs[k][...] = ready[place_ref[3 + k]]


def gather_kernel(levels, rows, place_ref, *refs):
    ins, out_ref, held = refs[:-2], refs[-2], refs[-1]
    n = len(ins)
    for k in range(n):
        held[place_ref[3 + k]] = ins[k][...]
    width = ins[0].shape[1]
    for c in range(3):
        for l in range(levels):
            out_ref[c, l] = jnp.concatenate(
                [held[s, c, :, l * rows : (l + 1) * rows] for s in range(n)], axis=1
            )


def shards(analysis, zonal_waves, meridional_waves, amplitude_codes):
    n = lax.axis_size("gx")
    place = lax.axis_index("gx")
    _, levels, rows, lon_total = analysis.shape
    lat_total = rows * n
    blocks = lon_total // LANES
    halves = SUBS // blocks
    half_rows = rows // halves
    length = half_rows + 2 * MARGIN
    width = lon_total // n
    total = levels * rows

    odd = place % 2
    first, last = analysis[:, :, :MARGIN], analysis[:, :, rows - MARGIN :]
    within = [(i, i ^ 1) for i in range(n)]
    between = [(i, ((i - 1) ^ 1) + 1) for i in range(1, n - 1)]
    inner = lax.ppermute(jnp.where(odd == 1, first, last), "gx", within)
    outer = lax.ppermute(jnp.where(odd == 1, last, first), "gx", between)

    order = [0]
    reach = n
    while reach > 1:
        order += range(reach // 2, reach)
        reach //= 2
    partners = jnp.stack([place ^ k for k in order])
    scalars = jnp.concatenate([jnp.stack([odd, place, jnp.int32(n)]), partners]).astype(jnp.int32)

    vmem = pl.BlockSpec(memory_space=pltpu.VMEM)
    smem = pl.BlockSpec(memory_space=pltpu.SMEM)
    anywhere = pl.BlockSpec(memory_space=pltpu.HBM)
    padded = -(-(rows + 2 * MARGIN) // LANES) * LANES
    modes = zonal_waves.shape[1]
    state_shape = jax.ShapeDtypeStruct((3 * levels, GROUPS, length * TILE, LANES), jnp.float32)
    start, added, coef, table = pl.pallas_call(
        functools.partial(prepare_kernel, lat_total, halves),
        out_shape=[
            state_shape,
            jax.ShapeDtypeStruct((levels, 2 * MARGIN, lon_total), jnp.float32),
            jax.ShapeDtypeStruct((3, GROUPS, length * TILE, LANES), jnp.float32),
            jax.ShapeDtypeStruct((2 * LANES, 2 * LANES), jnp.bfloat16),
        ],
        in_specs=[smem] + [anywhere] * 4,
        out_specs=[vmem] * 4,
        scratch_shapes=[
            pltpu.VMEM(analysis.shape, jnp.bfloat16),
            pltpu.VMEM(zonal_waves.shape, jnp.int32),
            pltpu.VMEM(zonal_waves.shape, jnp.int32),
            pltpu.VMEM(zonal_waves.shape, jnp.int32),
            pltpu.VMEM((levels, 2 * modes, lon_total), jnp.float32),
            pltpu.VMEM((levels, 2 * modes, padded), jnp.float32),
            pltpu.SemaphoreType.DMA((4,)),
        ],
        cost_estimate=pl.CostEstimate(flops=4_000_000, bytes_accessed=8_000_000, transcendentals=80_000),
        compiler_params=pltpu.CompilerParams(vmem_limit_bytes=12 * 1024 * 1024),
        name="prepare",
    )(scalars, *(pltpu.with_memory_space_constraint(x, pltpu.HBM) for x in (analysis, zonal_waves, meridional_waves, amplitude_codes)))

    piece = jax.ShapeDtypeStruct((3, width, total), jnp.bfloat16)
    *sent, _ = pl.pallas_call(
        functools.partial(member_kernel, levels, halves, blocks, rows),
        out_shape=[piece] * n + [state_shape],
        in_specs=[smem] + [vmem] * 6,
        out_specs=[vmem] * (n + 1),
        input_output_aliases={6: n},
        scratch_shapes=[
            pltpu.VMEM((3 * levels, GROUPS, length * TILE, LANES), jnp.float32),
            pltpu.VMEM((n, 3, width, total), jnp.bfloat16),
        ],
        compiler_params=pltpu.CompilerParams(vmem_limit_bytes=16 * 1024 * 1024),
        name="member_steps",
    )(scalars, inner, outer, added, coef, table, start)

    got = [sent[0]]
    for piece_of, k in list(zip(sent, order))[1:]:
        got.append(lax.ppermute(piece_of, "gx", [(i, i ^ k) for i in range(n)]))
    return pl.pallas_call(
        functools.partial(gather_kernel, levels, rows),
        out_shape=jax.ShapeDtypeStruct((3, levels, width, lat_total), jnp.bfloat16),
        in_specs=[smem] + [vmem] * n,
        out_specs=vmem,
        scratch_shapes=[pltpu.VMEM((n, 3, width, total), jnp.bfloat16)],
        compiler_params=pltpu.CompilerParams(vmem_limit_bytes=12 * 1024 * 1024),
        name="lay_out",
    )(scalars, *got)


def solution(mesh):
    placed = (P(None, None, "gx", None), P("member", None), P("member", None), P("member", None))
    return jax.shard_map(
        shards, mesh=mesh, in_specs=placed, out_specs=P("member", None, "gx", None), check_vma=False
    )
```

```python
import functools
import math

import jax
import jax.numpy as jnp
from jax import lax
from jax.experimental import pallas as pl
from jax.experimental.pallas import tpu as pltpu
from jax.sharding import PartitionSpec as P

NY = 1536
STEPS = 4
TIME_STEP = 0.15
FILTER = 0.03
GRAVITY = 0.5
AMP_UNIT = 0.04
LANES = 128
SUBS = 16
TILE = 8
GROUPS = SUBS // TILE
MARGIN = 2 * STEPS


def lon_operators():
    shape = (2 * LANES, 2 * LANES)
    row = lax.broadcasted_iota(jnp.int32, shape, 0)
    column = lax.broadcasted_iota(jnp.int32, shape, 1)
    at = jnp.where(row < LANES + 2, row, jnp.where(row >= 2 * LANES - 2, row - 2 * LANES, -LANES))
    reach = at - jnp.where(column < LANES, column, column - LANES)
    size = jnp.abs(reach)
    slopes = jnp.where(size == 1, 8.0, jnp.where(size == 2, -1.0, 0.0)) * jnp.where(reach > 0, 1.0, -1.0)
    smooths = jnp.where(size == 1, 4.0, jnp.where(size == 2, -1.0, 0.0))
    return jnp.where(column < LANES, slopes, smooths).astype(jnp.bfloat16)


def with_ends(x, halves, lane):
    ahead = pltpu.roll(x, SUBS - halves, 0)
    behind = pltpu.roll(x, halves, 0)
    return jnp.concatenate([x, jnp.where(lane < 2, ahead, behind)], axis=1)


def slope(p1, m1, p2, m2):
    return 8.0 * (p1 - m1) - (p2 - m2)


def level_sums(slopes):
    below = [None] * len(slopes)
    running = None
    for k in reversed(range(len(slopes))):
        running = slopes[k] if running is None else running + slopes[k]
        below[k] = running
    return [(0.5 * GRAVITY) * (running + b) for b in below]


def rows_of(ref, f, t):
    at = pl.ds(pl.multiple_of(t * TILE, TILE), TILE)
    return jnp.concatenate([ref[f, g, at, :] for g in range(GROUPS)], axis=0)


def step_rows(src, dst, coef, table, first, count, halves, levels):
    lane = lax.broadcasted_iota(jnp.int32, (SUBS, LANES), 1)
    gy = TIME_STEP / 12.0 / FILTER
    loaded = {}

    def get(f, k):
        if (f, k) not in loaded:
            loaded[f, k] = rows_of(src, f, first + k).astype(jnp.bfloat16)
        return loaded[f, k]

    flux = {}

    def north_flux(l, k):
        if (l, k) not in flux:
            v = get(2 * levels + l, k)
            flux[l, k] = v + get(l, k) * v
        return flux[l, k]

    def lon_parts(k):
        pieces = [with_ends(get(f, k), halves, lane) for f in range(3 * levels)]
        both = jnp.dot(jnp.concatenate(pieces, axis=0), table[...], preferred_element_type=jnp.float32)
        fluxes = []
        for l in range(levels):
            u = get(levels + l, k)
            fluxes.append(with_ends(u + get(l, k) * u, halves, lane))
        east = jnp.dot(jnp.concatenate(fluxes, axis=0), table[:, :LANES], preferred_element_type=jnp.float32)
        return both, east

    for k in range(count):
        t = first + k
        both, east_of = lon_parts(k)

        def parts(c, l):
            f = c * levels + l
            at = slice(f * SUBS, (f + 1) * SUBS)
            yp1, ym1, yp2, ym2 = (get(f, k + d) for d in (1, -1, 2, -2))
            ax = both[at, :LANES].astype(jnp.bfloat16)
            return ax, slope(yp1, ym1, yp2, ym2), 4.0 * (yp1 + ym1) - (yp2 + ym2), both[at, LANES:]

        def finish(c, l, smooth, change):
            f = c * levels + l
            change = smooth + change.astype(jnp.float32)
            new = (1.0 - 12.0 * FILTER) * rows_of(src, f, t) + FILTER * change
            at = pl.ds(pl.multiple_of(t * TILE, TILE), TILE)
            for g in range(GROUPS):
                dst[f, g, at, :] = new[g * TILE : (g + 1) * TILE]

        gx, gf = (rows_of(coef, i, t).astype(jnp.bfloat16) for i in range(2))
        hx, hy = [], []
        for l in range(levels):
            ax, ay, sy, sx = parts(0, l)
            hx.append(ax)
            hy.append(ay)
            east = east_of[l * SUBS : (l + 1) * SUBS].astype(jnp.bfloat16)
            north = slope(*(north_flux(l, k + d) for d in (1, -1, 2, -2)))
            finish(0, l, sx, sy - (gx * east + gy * north))
        px, py = level_sums(hx), level_sums(hy)
        for l in range(levels):
            u, v = get(levels + l, k), get(2 * levels + l, k)
            ax, ay, sy, sx = parts(1, l)
            finish(1, l, sx, sy - (gx * (u * ax + px[l]) + v * (gy * ay - gf)))
            ax, ay, sy, sx = parts(2, l)
            finish(2, l, sx, sy - (u * (gx * ax + gf) + gy * (v * ay + py[l])))


LARGEST_GROUP = 14


def group_of(count):
    return max(k for k in range(1, LARGEST_GROUP + 1) if count % k == 0)


def as_column(row):
    count = row.shape[1]
    square = jnp.broadcast_to(row, (count, count))
    here = lax.broadcasted_iota(jnp.int32, (count, count), 0) == lax.broadcasted_iota(jnp.int32, (count, count), 1)
    return jnp.sum(jnp.where(here, square, 0.0), axis=1, keepdims=True)


def waves(wave, cells, period):
    product = wave * cells
    left = product - jnp.floor(product * (1.0 / period)) * period
    left = jnp.where(left < 0.0, left + period, left)
    left = jnp.where(left >= period, left - period, left)
    quarter = jnp.floor(left * (4.0 / period) + 0.5)
    angle = (left - quarter * (period / 4.0)) * (2.0 * math.pi / period)
    square = angle * angle
    sine, cosine = 0.0, 0.0
    for k in (9, 7, 5, 3, 1):
        sine = sine * square + (-1.0) ** (k // 2) / math.factorial(k)
    for k in (10, 8, 6, 4, 2, 0):
        cosine = cosine * square + (-1.0) ** (k // 2) / math.factorial(k)
    sine = sine * angle
    odd = (quarter == 1.0) | (quarter == 3.0)
    cos_size, sin_size = jnp.where(odd, sine, cosine), jnp.where(odd, cosine, sine)
    cos_of = jnp.where((quarter == 1.0) | (quarter == 2.0), -cos_size, cos_size)
    sin_of = jnp.where((quarter == 2.0) | (quarter == 3.0), -sin_size, sin_size)
    return cos_of, sin_of


def put_rows(state, f, t, part, values, parts):
    for b in range(values.shape[1] // LANES):
        spot = b * parts + part
        at = pl.ds(t * TILE + spot % TILE, TILE, stride=TILE)
        state[f, spot // TILE, at, :] = values[:, b * LANES : (b + 1) * LANES]


def prepare_kernel(
    lat_total, halves, place_ref, analysis_ref, zonal_hbm, meridional_hbm, code_hbm,
    state, added_ref, coef, table,
    own_ref, zonal_ref, meridional_ref, code_ref, lon_ref, lat_ref, sems,
):
    copies = [
        pltpu.make_async_copy(source, target, sems.at[i])
        for i, (source, target) in enumerate(
            (
                (zonal_hbm, zonal_ref),
                (meridional_hbm, meridional_ref),
                (code_hbm, code_ref),
                (analysis_ref, own_ref),
            )
        )
    ]
    for copy in copies:
        copy.start()
    levels, modes = zonal_ref.shape
    rows = own_ref.shape[2]
    half_rows = rows // halves
    length = half_rows + 2 * MARGIN
    lon_total, padded = lon_ref.shape[2], lat_ref.shape[2]
    start = place_ref[1] * rows - MARGIN

    table[...] = lon_operators()
    part = lax.broadcasted_iota(jnp.int32, (SUBS, LANES), 0) % halves
    row = start + part * half_rows + lax.broadcasted_iota(jnp.int32, (SUBS, LANES), 1)
    latitude = math.pi / 3.0 * (2.0 * (row.astype(jnp.float32) + 0.5) / lat_total - 1.0)
    factors = (
        (TIME_STEP / 12.0 / FILTER) / jnp.cos(latitude),
        (2.0 * TIME_STEP / FILTER) * jnp.sin(latitude),
        ((row >= 0) & (row < lat_total)).astype(jnp.float32),
    )
    for which in range(3):
        for t in range(length):
            tile = jnp.broadcast_to(factors[which][:TILE, t : t + 1], (TILE, LANES))
            for g in range(GROUPS):
                coef[which, g, t * TILE : (t + 1) * TILE, :] = tile

    lon_cells = lax.broadcasted_iota(jnp.int32, (modes, lon_total), 1).astype(jnp.float32)
    cell = lax.broadcasted_iota(jnp.int32, (modes, padded), 1) + start
    inside = (cell >= 0) & (cell < lat_total)
    lat_cells = jnp.where(inside, cell, 0).astype(jnp.float32)
    for copy in copies[:3]:
        copy.wait()
    for l in range(levels):
        zonal, meridional, code = (
            as_column(r[l : l + 1, :].astype(jnp.float32)) for r in (zonal_ref, meridional_ref, code_ref)
        )
        weight = AMP_UNIT * code
        cos_of, sin_of = waves(zonal, lon_cells, lon_total)
        lon_ref[l, :modes, :] = weight * cos_of
        lon_ref[l, modes:, :] = -weight * sin_of
        cos_of, sin_of = waves(meridional, lat_cells, lat_total)
        lat_ref[l, :modes, :] = jnp.where(inside, cos_of, 0.0)
        lat_ref[l, modes:, :] = jnp.where(inside, sin_of, 0.0)

    copies[3].wait()

    def load(l, carry):
        added = lax.dot_general(
            lat_ref[l], lon_ref[l], (((0,), (0,)), ((), ())),
            precision=lax.Precision.HIGHEST, preferred_element_type=jnp.float32,
        )
        added_ref[l, :MARGIN, :] = added[:MARGIN]
        added_ref[l, MARGIN:, :] = added[rows + MARGIN : rows + 2 * MARGIN]
        for c in range(3):
            own = own_ref[c, l].astype(jnp.float32)
            if c == 0:
                own = (own + added[MARGIN : rows + MARGIN]).astype(jnp.bfloat16).astype(jnp.float32)
            for half in range(halves):
                for t in range(0, length, TILE):
                    at = half * half_rows + t - MARGIN
                    if 0 <= at < rows:
                        put_rows(state, c * levels + l, t, half, own[at : at + TILE], halves)
        return carry

    lax.fori_loop(0, levels, load, 0, unroll=True)


def member_kernel(levels, halves, blocks, rows, place_ref, inner_ref, outer_ref, added_ref, coef, table, _, *rest):
    outs, one, (two, ready) = rest[:-3], rest[-3], rest[-2:]
    half_rows = rows // halves
    length = half_rows + 2 * MARGIN
    odd = place_ref[0] == 1

    def load(l, carry):
        for c in range(3):
            inner, outer = (r[c, l].astype(jnp.float32) for r in (inner_ref, outer_ref))
            low, high = jnp.where(odd, inner, outer), jnp.where(odd, outer, inner)
            if c == 0:
                low = (low + added_ref[l, :MARGIN, :]).astype(jnp.bfloat16).astype(jnp.float32)
                high = (high + added_ref[l, MARGIN:, :]).astype(jnp.bfloat16).astype(jnp.float32)
            put_rows(one, c * levels + l, 0, 0, low, halves)
            put_rows(one, c * levels + l, length - MARGIN, halves - 1, high, halves)
        return carry

    lax.fori_loop(0, levels, load, 0)

    src, dst = one, two
    for step in range(STEPS):
        begin = 2 * (step + 1)
        count = length - 2 * begin

        group = group_of(count)

        def body(i, carry, src=src, dst=dst, begin=begin, group=group):
            step_rows(src, dst, coef, table, begin + i * group, group, halves, levels)
            return carry

        lax.fori_loop(0, count // group, body, 0)
        if step < STEPS - 1:
            @pl.when((place_ref[1] == 0) | (place_ref[1] == place_ref[2] - 1))
            def _(dst=dst, begin=begin):
                def clear(f, carry):
                    for t in list(range(begin, MARGIN)) + list(range(length - MARGIN, length - begin)):
                        at = slice(t * TILE, (t + 1) * TILE)
                        for g in range(GROUPS):
                            dst[f, g, at, :] = jnp.where(coef[2, g, at, :] > 0.5, dst[f, g, at, :], 0.0)
                    return carry

                lax.fori_loop(0, 3 * levels, clear, 0)
        src, dst = dst, src

    total = levels * rows
    per = len(outs)
    width = blocks * LANES // per
    for c in range(3):
        for b in range(blocks):
            tiles = []
            for l in range(levels):
                for half in range(halves):
                    for t in range(MARGIN, MARGIN + half_rows, TILE):
                        spot = b * halves + half
                        at = pl.ds(t * TILE + spot % TILE, TILE, stride=TILE)
                        tiles.append(src[c * levels + l, spot // TILE, at, :])
            for j in range(total // LANES):
                square = jnp.concatenate(tiles[j * (LANES // TILE) : (j + 1) * (LANES // TILE)], axis=0)
                turned = square.T.astype(jnp.bfloat16)
                for d in range(LANES // width):
                    ready[b * (LANES // width) + d, c, :, j * LANES : (j + 1) * LANES] = turned[d * width : (d + 1) * width]
    for k in range(per):
        outs[k][...] = ready[place_ref[3 + k]]


def gather_kernel(levels, rows, place_ref, *refs):
    ins, out_ref, held = refs[:-2], refs[-2], refs[-1]
    n = len(ins)
    for k in range(n):
        held[place_ref[3 + k]] = ins[k][...]
    width = ins[0].shape[1]
    for c in range(3):
        for l in range(levels):
            out_ref[c, l] = jnp.concatenate(
                [held[s, c, :, l * rows : (l + 1) * rows] for s in range(n)], axis=1
            )


def exchange_order(n):
    pairs = [(k, k + 1) for k in range(2, n, 2)]
    far = [p for p in reversed(pairs) if p[0] >= n // 2]
    near = [p for p in pairs if n // 4 <= p[0] < n // 2] + [p for p in reversed(pairs) if p[0] < n // 4]
    woven = far[:2]
    for k in range(max(len(far), len(near))):
        woven += near[k : k + 1] + far[k + 2 : k + 3]
    return [0] + [k for p in woven for k in p] + [1]


def shards(analysis, zonal_waves, meridional_waves, amplitude_codes):
    n = lax.axis_size("gx")
    place = lax.axis_index("gx")
    _, levels, rows, lon_total = analysis.shape
    lat_total = rows * n
    blocks = lon_total // LANES
    halves = SUBS // blocks
    half_rows = rows // halves
    length = half_rows + 2 * MARGIN
    width = lon_total // n
    total = levels * rows

    odd = place % 2
    first, last = analysis[:, :, :MARGIN], analysis[:, :, rows - MARGIN :]
    within = [(i, i ^ 1) for i in range(n)]
    between = [(i, ((i - 1) ^ 1) + 1) for i in range(1, n - 1)]
    inner = lax.ppermute(jnp.where(odd == 1, first, last), "gx", within)
    outer = lax.ppermute(jnp.where(odd == 1, last, first), "gx", between)

    order = exchange_order(n)
    partners = jnp.stack([place ^ k for k in order])
    scalars = jnp.concatenate([jnp.stack([odd, place, jnp.int32(n)]), partners]).astype(jnp.int32)

    vmem = pl.BlockSpec(memory_space=pltpu.VMEM)
    smem = pl.BlockSpec(memory_space=pltpu.SMEM)
    anywhere = pl.BlockSpec(memory_space=pltpu.HBM)
    padded = -(-(rows + 2 * MARGIN) // LANES) * LANES
    modes = zonal_waves.shape[1]
    state_shape = jax.ShapeDtypeStruct((3 * levels, GROUPS, length * TILE, LANES), jnp.float32)
    start, added, coef, table = pl.pallas_call(
        functools.partial(prepare_kernel, lat_total, halves),
        out_shape=[
            state_shape,
            jax.ShapeDtypeStruct((levels, 2 * MARGIN, lon_total), jnp.float32),
            jax.ShapeDtypeStruct((3, GROUPS, length * TILE, LANES), jnp.float32),
            jax.ShapeDtypeStruct((2 * LANES, 2 * LANES), jnp.bfloat16),
        ],
        in_specs=[smem] + [anywhere] * 4,
        out_specs=[vmem] * 4,
        scratch_shapes=[
            pltpu.VMEM(analysis.shape, jnp.bfloat16),
            pltpu.VMEM(zonal_waves.shape, jnp.int32),
            pltpu.VMEM(zonal_waves.shape, jnp.int32),
            pltpu.VMEM(zonal_waves.shape, jnp.int32),
            pltpu.VMEM((levels, 2 * modes, lon_total), jnp.float32),
            pltpu.VMEM((levels, 2 * modes, padded), jnp.float32),
            pltpu.SemaphoreType.DMA((4,)),
        ],
        cost_estimate=pl.CostEstimate(flops=4_000_000, bytes_accessed=8_000_000, transcendentals=80_000),
        compiler_params=pltpu.CompilerParams(vmem_limit_bytes=12 * 1024 * 1024),
        name="prepare",
    )(scalars, *(pltpu.with_memory_space_constraint(x, pltpu.HBM) for x in (analysis, zonal_waves, meridional_waves, amplitude_codes)))

    piece = jax.ShapeDtypeStruct((3, width, total), jnp.bfloat16)
    *sent, _ = pl.pallas_call(
        functools.partial(member_kernel, levels, halves, blocks, rows),
        out_shape=[piece] * n + [state_shape],
        in_specs=[smem] + [vmem] * 6,
        out_specs=[vmem] * (n + 1),
        input_output_aliases={6: n},
        scratch_shapes=[
            pltpu.VMEM((3 * levels, GROUPS, length * TILE, LANES), jnp.float32),
            pltpu.VMEM((n, 3, width, total), jnp.bfloat16),
        ],
        compiler_params=pltpu.CompilerParams(vmem_limit_bytes=16 * 1024 * 1024),
        name="member_steps",
    )(scalars, inner, outer, added, coef, table, start)

    got = [sent[0]]
    for piece_of, k in list(zip(sent, order))[1:]:
        got.append(lax.ppermute(piece_of, "gx", [(i, i ^ k) for i in range(n)]))
    return pl.pallas_call(
        functools.partial(gather_kernel, levels, rows),
        out_shape=jax.ShapeDtypeStruct((3, levels, width, lat_total), jnp.bfloat16),
        in_specs=[smem] + [vmem] * n,
        out_specs=vmem,
        scratch_shapes=[pltpu.VMEM((n, 3, width, total), jnp.bfloat16)],
        compiler_params=pltpu.CompilerParams(vmem_limit_bytes=12 * 1024 * 1024),
        name="lay_out",
    )(scalars, *got)


def solution(mesh):
    placed = (P(None, None, "gx", None), P("member", None), P("member", None), P("member", None))
    return jax.shard_map(
        shards, mesh=mesh, in_specs=placed, out_specs=P("member", None, "gx", None), check_vma=False
    )
```

```python
import functools
import math

import jax
import jax.numpy as jnp
from jax import lax
from jax.experimental import pallas as pl
from jax.experimental.pallas import tpu as pltpu
from jax.sharding import PartitionSpec as P

NY = 1536
STEPS = 4
TIME_STEP = 0.15
FILTER = 0.03
GRAVITY = 0.5
AMP_UNIT = 0.04
LANES = 128
SUBS = 16
TILE = 8
GROUPS = SUBS // TILE
MARGIN = 2 * STEPS


def lon_operators():
    shape = (2 * LANES, 2 * LANES)
    row = lax.broadcasted_iota(jnp.int32, shape, 0)
    column = lax.broadcasted_iota(jnp.int32, shape, 1)
    at = jnp.where(row < LANES + 2, row, jnp.where(row >= 2 * LANES - 2, row - 2 * LANES, -LANES))
    reach = at - jnp.where(column < LANES, column, column - LANES)
    size = jnp.abs(reach)
    slopes = jnp.where(size == 1, 8.0, jnp.where(size == 2, -1.0, 0.0)) * jnp.where(reach > 0, 1.0, -1.0)
    smooths = jnp.where(size == 0, -12.0, jnp.where(size == 1, 4.0, jnp.where(size == 2, -1.0, 0.0)))
    return jnp.where(column < LANES, slopes, smooths).astype(jnp.bfloat16)


def with_ends(x, halves, lane):
    ahead = pltpu.roll(x, SUBS - halves, 0)
    behind = pltpu.roll(x, halves, 0)
    return jnp.concatenate([x, jnp.where(lane < 2, ahead, behind)], axis=1)


def slope(p1, m1, p2, m2):
    return 8.0 * (p1 - m1) - (p2 - m2)


def level_sums(slopes):
    below = [None] * len(slopes)
    running = None
    for k in reversed(range(len(slopes))):
        running = slopes[k] if running is None else running + slopes[k]
        below[k] = running
    return [(0.5 * GRAVITY) * (running + b) for b in below]


def rows_of(ref, f, t):
    at = pl.ds(pl.multiple_of(t * TILE, TILE), TILE)
    return jnp.concatenate([ref[f, g, at, :] for g in range(GROUPS)], axis=0)


def step_rows(src, dst, coef, table, first, count, halves, levels):
    lane = lax.broadcasted_iota(jnp.int32, (SUBS, LANES), 1)
    gy = TIME_STEP / 12.0 / FILTER
    loaded = {}

    def get(f, k):
        if (f, k) not in loaded:
            loaded[f, k] = rows_of(src, f, first + k).astype(jnp.bfloat16)
        return loaded[f, k]

    flux = {}

    def north_flux(l, k):
        if (l, k) not in flux:
            v = get(2 * levels + l, k)
            flux[l, k] = v + get(l, k) * v
        return flux[l, k]

    def lon_parts(k):
        pieces = [with_ends(get(f, k), halves, lane) for f in range(3 * levels)]
        both = jnp.dot(jnp.concatenate(pieces, axis=0), table[...], preferred_element_type=jnp.float32)
        fluxes = []
        for l in range(levels):
            u = get(levels + l, k)
            fluxes.append(with_ends(u + get(l, k) * u, halves, lane))
        east = jnp.dot(jnp.concatenate(fluxes, axis=0), table[:, :LANES], preferred_element_type=jnp.float32)
        return both, east

    for k in range(count):
        t = first + k
        both, east_of = lon_parts(k)

        def parts(c, l):
            f = c * levels + l
            at = slice(f * SUBS, (f + 1) * SUBS)
            yp1, ym1, yp2, ym2 = (get(f, k + d) for d in (1, -1, 2, -2))
            ax = both[at, :LANES].astype(jnp.bfloat16)
            return ax, slope(yp1, ym1, yp2, ym2), 4.0 * (yp1 + ym1) - (yp2 + ym2), both[at, LANES:]

        def finish(c, l, smooth, change):
            f = c * levels + l
            change = smooth + change.astype(jnp.float32)
            new = rows_of(src, f, t) + FILTER * change
            at = pl.ds(pl.multiple_of(t * TILE, TILE), TILE)
            for g in range(GROUPS):
                dst[f, g, at, :] = new[g * TILE : (g + 1) * TILE]

        gx, gf = (rows_of(coef, i, t).astype(jnp.bfloat16) for i in range(2))
        hx, hy = [], []
        for l in range(levels):
            ax, ay, sy, sx = parts(0, l)
            hx.append(ax)
            hy.append(ay)
            east = east_of[l * SUBS : (l + 1) * SUBS].astype(jnp.bfloat16)
            north = slope(*(north_flux(l, k + d) for d in (1, -1, 2, -2)))
            finish(0, l, sx, sy - (gx * east + gy * north))
        px, py = level_sums(hx), level_sums(hy)
        for l in range(levels):
            u, v = get(levels + l, k), get(2 * levels + l, k)
            ax, ay, sy, sx = parts(1, l)
            finish(1, l, sx, sy - (gx * (u * ax + px[l]) + v * (gy * ay - gf)))
            ax, ay, sy, sx = parts(2, l)
            finish(2, l, sx, sy - (u * (gx * ax + gf) + gy * (v * ay + py[l])))


LARGEST_GROUP = 18


def group_of(count):
    return max(k for k in range(1, LARGEST_GROUP + 1) if count % k == 0)


def as_column(row):
    count = row.shape[1]
    square = jnp.broadcast_to(row, (count, count))
    here = lax.broadcasted_iota(jnp.int32, (count, count), 0) == lax.broadcasted_iota(jnp.int32, (count, count), 1)
    return jnp.sum(jnp.where(here, square, 0.0), axis=1, keepdims=True)


def waves(wave, cells, period):
    product = wave * cells
    left = product - jnp.floor(product * (1.0 / period)) * period
    left = jnp.where(left < 0.0, left + period, left)
    left = jnp.where(left >= period, left - period, left)
    quarter = jnp.floor(left * (4.0 / period) + 0.5)
    angle = (left - quarter * (period / 4.0)) * (2.0 * math.pi / period)
    square = angle * angle
    sine, cosine = 0.0, 0.0
    for k in (9, 7, 5, 3, 1):
        sine = sine * square + (-1.0) ** (k // 2) / math.factorial(k)
    for k in (10, 8, 6, 4, 2, 0):
        cosine = cosine * square + (-1.0) ** (k // 2) / math.factorial(k)
    sine = sine * angle
    odd = (quarter == 1.0) | (quarter == 3.0)
    cos_size, sin_size = jnp.where(odd, sine, cosine), jnp.where(odd, cosine, sine)
    cos_of = jnp.where((quarter == 1.0) | (quarter == 2.0), -cos_size, cos_size)
    sin_of = jnp.where((quarter == 2.0) | (quarter == 3.0), -sin_size, sin_size)
    return cos_of, sin_of


def split(table, parts):
    lead = table.astype(jnp.bfloat16)
    rest = (table - lead.astype(jnp.float32)).astype(jnp.bfloat16)
    return jnp.concatenate([(lead, rest)[part] for part in parts], axis=0)


def put_rows(state, f, t, part, values, parts):
    for b in range(values.shape[1] // LANES):
        spot = b * parts + part
        at = pl.ds(t * TILE + spot % TILE, TILE, stride=TILE)
        state[f, spot // TILE, at, :] = values[:, b * LANES : (b + 1) * LANES]


def prepare_kernel(
    lat_total, halves, place_ref, analysis_ref, zonal_hbm, meridional_hbm, code_hbm,
    state, added_ref, coef, table,
    own_ref, zonal_ref, meridional_ref, code_ref, lon_ref, lat_ref, sems,
):
    copies = [
        pltpu.make_async_copy(source, target, sems.at[i])
        for i, (source, target) in enumerate(
            (
                (zonal_hbm, zonal_ref),
                (meridional_hbm, meridional_ref),
                (code_hbm, code_ref),
                (analysis_ref, own_ref),
            )
        )
    ]
    for copy in copies:
        copy.start()
    levels, modes = zonal_ref.shape
    rows = own_ref.shape[2]
    half_rows = rows // halves
    length = half_rows + 2 * MARGIN
    lon_total, padded = lon_ref.shape[2], lat_ref.shape[2]
    start = place_ref[1] * rows - MARGIN

    table[...] = lon_operators()
    part = lax.broadcasted_iota(jnp.int32, (SUBS, LANES), 0) % halves
    row = start + part * half_rows + lax.broadcasted_iota(jnp.int32, (SUBS, LANES), 1)
    latitude = math.pi / 3.0 * (2.0 * (row.astype(jnp.float32) + 0.5) / lat_total - 1.0)
    factors = (
        (TIME_STEP / 12.0 / FILTER) / jnp.cos(latitude),
        (2.0 * TIME_STEP / FILTER) * jnp.sin(latitude),
        ((row >= 0) & (row < lat_total)).astype(jnp.float32),
    )
    for which in range(3):
        for t in range(length):
            tile = jnp.broadcast_to(factors[which][:TILE, t : t + 1], (TILE, LANES))
            for g in range(GROUPS):
                coef[which, g, t * TILE : (t + 1) * TILE, :] = tile

    lon_cells = lax.broadcasted_iota(jnp.int32, (modes, lon_total), 1).astype(jnp.float32)
    cell = lax.broadcasted_iota(jnp.int32, (modes, padded), 1) + start
    lat_cells = jnp.where((cell >= 0) & (cell < lat_total), cell, 0).astype(jnp.float32)
    cell = lax.broadcasted_iota(jnp.int32, (2 * modes, padded), 1) + start
    inside = (cell >= 0) & (cell < lat_total)
    for copy in copies[:3]:
        copy.wait()
    for l in range(levels):
        zonal, meridional, code = (
            as_column(r[l : l + 1, :].astype(jnp.float32)) for r in (zonal_ref, meridional_ref, code_ref)
        )
        weight = AMP_UNIT * code
        cos_of, sin_of = waves(zonal, lon_cells, lon_total)
        lon_ref[l] = split(jnp.concatenate([weight * cos_of, -weight * sin_of], axis=0), (0, 1, 0))
        cos_of, sin_of = waves(meridional, lat_cells, lat_total)
        lat_waves = jnp.concatenate([cos_of, sin_of], axis=0)
        lat_ref[l] = split(jnp.where(inside, lat_waves, 0.0), (0, 0, 1))

    copies[3].wait()

    def load(l, carry):
        added = lax.dot_general(
            lat_ref[l], lon_ref[l], (((0,), (0,)), ((), ())), preferred_element_type=jnp.float32
        )
        added_ref[l, :MARGIN, :] = added[:MARGIN]
        added_ref[l, MARGIN:, :] = added[rows + MARGIN : rows + 2 * MARGIN]
        for c in range(3):
            own = own_ref[c, l].astype(jnp.float32)
            if c == 0:
                own = (own + added[MARGIN : rows + MARGIN]).astype(jnp.bfloat16).astype(jnp.float32)
            for half in range(halves):
                for t in range(0, length, TILE):
                    at = half * half_rows + t - MARGIN
                    if 0 <= at < rows:
                        put_rows(state, c * levels + l, t, half, own[at : at + TILE], halves)
        return carry

    lax.fori_loop(0, levels, load, 0, unroll=True)


def member_kernel(levels, halves, blocks, rows, place_ref, inner_ref, outer_ref, added_ref, coef, table, _, *rest):
    outs, one, (two, ready) = rest[:-3], rest[-3], rest[-2:]
    half_rows = rows // halves
    length = half_rows + 2 * MARGIN
    odd = place_ref[0] == 1

    def load(l, carry):
        for c in range(3):
            inner, outer = (r[c, l].astype(jnp.float32) for r in (inner_ref, outer_ref))
            low, high = jnp.where(odd, inner, outer), jnp.where(odd, outer, inner)
            if c == 0:
                low = (low + added_ref[l, :MARGIN, :]).astype(jnp.bfloat16).astype(jnp.float32)
                high = (high + added_ref[l, MARGIN:, :]).astype(jnp.bfloat16).astype(jnp.float32)
            put_rows(one, c * levels + l, 0, 0, low, halves)
            put_rows(one, c * levels + l, length - MARGIN, halves - 1, high, halves)
        return carry

    lax.fori_loop(0, levels, load, 0)

    src, dst = one, two
    for step in range(STEPS):
        begin = 2 * (step + 1)
        count = length - 2 * begin

        group = group_of(count)

        def body(i, carry, src=src, dst=dst, begin=begin, group=group):
            step_rows(src, dst, coef, table, begin + i * group, group, halves, levels)
            return carry

        lax.fori_loop(0, count // group, body, 0)
        if step < STEPS - 1:
            @pl.when((place_ref[1] == 0) | (place_ref[1] == place_ref[2] - 1))
            def _(dst=dst, begin=begin):
                def clear(f, carry):
                    for t in list(range(begin, MARGIN)) + list(range(length - MARGIN, length - begin)):
                        at = slice(t * TILE, (t + 1) * TILE)
                        for g in range(GROUPS):
                            dst[f, g, at, :] = jnp.where(coef[2, g, at, :] > 0.5, dst[f, g, at, :], 0.0)
                    return carry

                lax.fori_loop(0, 3 * levels, clear, 0)
        src, dst = dst, src

    total = levels * rows
    per = len(outs)
    width = blocks * LANES // per
    for c in range(3):
        for b in range(blocks):
            tiles = []
            for l in range(levels):
                for half in range(halves):
                    for t in range(MARGIN, MARGIN + half_rows, TILE):
                        spot = b * halves + half
                        at = pl.ds(t * TILE + spot % TILE, TILE, stride=TILE)
                        tiles.append(src[c * levels + l, spot // TILE, at, :])
            for j in range(total // LANES):
                square = jnp.concatenate(tiles[j * (LANES // TILE) : (j + 1) * (LANES // TILE)], axis=0)
                turned = square.astype(jnp.bfloat16).T
                for d in range(LANES // width):
                    ready[b * (LANES // width) + d, c, :, j * LANES : (j + 1) * LANES] = turned[d * width : (d + 1) * width]
    for k in range(per):
        outs[k][...] = ready[place_ref[3 + k]]


def gather_kernel(levels, rows, place_ref, *refs):
    ins, (out_ref, held, laid, sems) = refs[:-4], refs[-4:]
    n = len(ins)
    copies = []
    for c in range(3):
        for k in range(n):
            held[place_ref[3 + k], c] = ins[k][c]
        for l in range(levels):
            laid[c, l] = jnp.concatenate([held[s, c, :, l * rows : (l + 1) * rows] for s in range(n)], axis=1)
            copies.append(pltpu.make_async_copy(laid.at[c, l], out_ref.at[c, l], sems.at[len(copies)]))
            copies[-1].start()
    for copy in copies:
        copy.wait()


def exchange_order(n):
    pairs = [(k, k + 1) for k in range(2, n, 2)]
    far = [p for p in reversed(pairs) if p[0] >= n // 2]
    near = [p for p in pairs if n // 4 <= p[0] < n // 2] + [p for p in reversed(pairs) if p[0] < n // 4]
    woven = far[:2]
    for k in range(max(len(far), len(near))):
        woven += near[k : k + 1] + far[k + 2 : k + 3]
    return [0] + [k for p in woven for k in p] + [1]


def shards(analysis, zonal_waves, meridional_waves, amplitude_codes):
    n = lax.axis_size("gx")
    place = lax.axis_index("gx")
    _, levels, rows, lon_total = analysis.shape
    lat_total = rows * n
    blocks = lon_total // LANES
    halves = SUBS // blocks
    half_rows = rows // halves
    length = half_rows + 2 * MARGIN
    width = lon_total // n
    total = levels * rows

    odd = place % 2
    first, last = analysis[:, :, :MARGIN], analysis[:, :, rows - MARGIN :]
    within = [(i, i ^ 1) for i in range(n)]
    between = [(i, ((i - 1) ^ 1) + 1) for i in range(1, n - 1)]
    inner = lax.ppermute(jnp.where(odd == 1, first, last), "gx", within)
    outer = lax.ppermute(jnp.where(odd == 1, last, first), "gx", between)

    order = exchange_order(n)
    partners = jnp.stack([place ^ k for k in order])
    scalars = jnp.concatenate([jnp.stack([odd, place, jnp.int32(n)]), partners]).astype(jnp.int32)

    vmem = pl.BlockSpec(memory_space=pltpu.VMEM)
    smem = pl.BlockSpec(memory_space=pltpu.SMEM)
    anywhere = pl.BlockSpec(memory_space=pltpu.HBM)
    padded = -(-(rows + 2 * MARGIN) // LANES) * LANES
    modes = zonal_waves.shape[1]
    state_shape = jax.ShapeDtypeStruct((3 * levels, GROUPS, length * TILE, LANES), jnp.float32)
    start, added, coef, table = pl.pallas_call(
        functools.partial(prepare_kernel, lat_total, halves),
        out_shape=[
            state_shape,
            jax.ShapeDtypeStruct((levels, 2 * MARGIN, lon_total), jnp.float32),
            jax.ShapeDtypeStruct((3, GROUPS, length * TILE, LANES), jnp.float32),
            jax.ShapeDtypeStruct((2 * LANES, 2 * LANES), jnp.bfloat16),
        ],
        in_specs=[smem] + [anywhere] * 4,
        out_specs=[vmem] * 4,
        scratch_shapes=[
            pltpu.VMEM(analysis.shape, jnp.bfloat16),
            pltpu.VMEM(zonal_waves.shape, jnp.int32),
            pltpu.VMEM(zonal_waves.shape, jnp.int32),
            pltpu.VMEM(zonal_waves.shape, jnp.int32),
            pltpu.VMEM((levels, 6 * modes, lon_total), jnp.bfloat16),
            pltpu.VMEM((levels, 6 * modes, padded), jnp.bfloat16),
            pltpu.SemaphoreType.DMA((4,)),
        ],
        cost_estimate=pl.CostEstimate(flops=4_000_000, bytes_accessed=8_000_000, transcendentals=80_000),
        compiler_params=pltpu.CompilerParams(vmem_limit_bytes=12 * 1024 * 1024),
        name="prepare",
    )(scalars, *(pltpu.with_memory_space_constraint(x, pltpu.HBM) for x in (analysis, zonal_waves, meridional_waves, amplitude_codes)))

    piece = jax.ShapeDtypeStruct((3, width, total), jnp.bfloat16)
    *sent, _ = pl.pallas_call(
        functools.partial(member_kernel, levels, halves, blocks, rows),
        out_shape=[piece] * n + [state_shape],
        in_specs=[smem] + [vmem] * 6,
        out_specs=[vmem] * (n + 1),
        input_output_aliases={6: n},
        scratch_shapes=[
            pltpu.VMEM((3 * levels, GROUPS, length * TILE, LANES), jnp.float32),
            pltpu.VMEM((n, 3, width, total), jnp.bfloat16),
        ],
        compiler_params=pltpu.CompilerParams(vmem_limit_bytes=16 * 1024 * 1024),
        name="member_steps",
    )(scalars, inner, outer, added, coef, table, start)

    got = [sent[0]]
    for piece_of, k in list(zip(sent, order))[1:]:
        got.append(lax.ppermute(piece_of, "gx", [(i, i ^ k) for i in range(n)]))
    return pl.pallas_call(
        functools.partial(gather_kernel, levels, rows),
        out_shape=jax.ShapeDtypeStruct((3, levels, width, lat_total), jnp.bfloat16),
        in_specs=[smem] + [vmem] * n,
        out_specs=pl.BlockSpec(memory_space=pl.ANY),
        scratch_shapes=[
            pltpu.VMEM((n, 3, width, total), jnp.bfloat16),
            pltpu.VMEM((3, levels, width, lat_total), jnp.bfloat16),
            pltpu.SemaphoreType.DMA((3 * levels,)),
        ],
        compiler_params=pltpu.CompilerParams(vmem_limit_bytes=12 * 1024 * 1024),
        name="lay_out",
    )(scalars, *got)


def solution(mesh):
    placed = (P(None, None, "gx", None), P("member", None), P("member", None), P("member", None))
    return jax.shard_map(
        shards, mesh=mesh, in_specs=placed, out_specs=P("member", None, "gx", None), check_vma=False
    )
```

```python
import functools
import math

import jax
import jax.numpy as jnp
from jax import lax
from jax.experimental import pallas as pl
from jax.experimental.pallas import tpu as pltpu
from jax.sharding import PartitionSpec as P

NY = 1536
STEPS = 4
TIME_STEP = 0.15
FILTER = 0.03
GRAVITY = 0.5
AMP_UNIT = 0.04
LANES = 128
SUBS = 16
TILE = 8
GROUPS = SUBS // TILE
MARGIN = 2 * STEPS


def lon_operators():
    shape = (2 * LANES, 2 * LANES)
    row = lax.broadcasted_iota(jnp.int32, shape, 0)
    column = lax.broadcasted_iota(jnp.int32, shape, 1)
    at = jnp.where(row < LANES + 2, row, jnp.where(row >= 2 * LANES - 2, row - 2 * LANES, -LANES))
    reach = at - jnp.where(column < LANES, column, column - LANES)
    size = jnp.abs(reach)
    slopes = jnp.where(size == 1, 8.0, jnp.where(size == 2, -1.0, 0.0)) * jnp.where(reach > 0, 1.0, -1.0)
    smooths = jnp.where(size == 0, -12.0, jnp.where(size == 1, 4.0, jnp.where(size == 2, -1.0, 0.0)))
    return jnp.where(column < LANES, slopes, smooths).astype(jnp.bfloat16)


def with_ends(x, halves, lane):
    ahead = pltpu.roll(x, SUBS - halves, 0)
    behind = pltpu.roll(x, halves, 0)
    return jnp.concatenate([x, jnp.where(lane < 2, ahead, behind)], axis=1)


def slope(p1, m1, p2, m2):
    return 8.0 * (p1 - m1) - (p2 - m2)


def level_sums(slopes):
    below = [None] * len(slopes)
    running = None
    for k in reversed(range(len(slopes))):
        running = slopes[k] if running is None else running + slopes[k]
        below[k] = running
    return [(0.5 * GRAVITY) * (running + b) for b in below]


def rows_of(ref, f, t):
    at = pl.ds(pl.multiple_of(t * TILE, TILE), TILE)
    return jnp.concatenate([ref[f, g, at, :] for g in range(GROUPS)], axis=0)


def step_rows(src, dst, coef, table, first, count, halves, levels):
    lane = lax.broadcasted_iota(jnp.int32, (SUBS, LANES), 1)
    gy = TIME_STEP / 12.0 / FILTER
    loaded = {}

    def get(f, k):
        if (f, k) not in loaded:
            loaded[f, k] = rows_of(src, f, first + k).astype(jnp.bfloat16)
        return loaded[f, k]

    flux = {}

    def north_flux(l, k):
        if (l, k) not in flux:
            v = get(2 * levels + l, k)
            flux[l, k] = v + get(l, k) * v
        return flux[l, k]

    def lon_parts(k):
        pieces = [with_ends(get(f, k), halves, lane) for f in range(3 * levels)]
        both = jnp.dot(jnp.concatenate(pieces, axis=0), table[...], preferred_element_type=jnp.float32)
        fluxes = []
        for l in range(levels):
            u = get(levels + l, k)
            fluxes.append(with_ends(u + get(l, k) * u, halves, lane))
        east = jnp.dot(jnp.concatenate(fluxes, axis=0), table[:, :LANES], preferred_element_type=jnp.float32)
        return both, east

    for k in range(count):
        t = first + k
        both, east_of = lon_parts(k)

        def parts(c, l):
            f = c * levels + l
            at = slice(f * SUBS, (f + 1) * SUBS)
            yp1, ym1, yp2, ym2 = (get(f, k + d) for d in (1, -1, 2, -2))
            ax = both[at, :LANES].astype(jnp.bfloat16)
            return ax, slope(yp1, ym1, yp2, ym2), 4.0 * (yp1 + ym1) - (yp2 + ym2), both[at, LANES:]

        def finish(c, l, smooth, change):
            f = c * levels + l
            change = smooth + change.astype(jnp.float32)
            new = rows_of(src, f, t) + FILTER * change
            at = pl.ds(pl.multiple_of(t * TILE, TILE), TILE)
            for g in range(GROUPS):
                dst[f, g, at, :] = new[g * TILE : (g + 1) * TILE]

        gx, gf = (rows_of(coef, i, t).astype(jnp.bfloat16) for i in range(2))
        hx, hy = [], []
        for l in range(levels):
            ax, ay, sy, sx = parts(0, l)
            hx.append(ax)
            hy.append(ay)
            east = east_of[l * SUBS : (l + 1) * SUBS].astype(jnp.bfloat16)
            north = slope(*(north_flux(l, k + d) for d in (1, -1, 2, -2)))
            finish(0, l, sx, sy - (gx * east + gy * north))
        px, py = level_sums(hx), level_sums(hy)
        for l in range(levels):
            u, v = get(levels + l, k), get(2 * levels + l, k)
            ax, ay, sy, sx = parts(1, l)
            finish(1, l, sx, sy - (gx * (u * ax + px[l]) + v * (gy * ay - gf)))
            ax, ay, sy, sx = parts(2, l)
            finish(2, l, sx, sy - (u * (gx * ax + gf) + gy * (v * ay + py[l])))


LARGEST_GROUP = 18


def group_of(count):
    return max(k for k in range(1, LARGEST_GROUP + 1) if count % k == 0)


def as_column(row):
    count = row.shape[1]
    square = jnp.broadcast_to(row, (count, count))
    here = lax.broadcasted_iota(jnp.int32, (count, count), 0) == lax.broadcasted_iota(jnp.int32, (count, count), 1)
    return jnp.sum(jnp.where(here, square, 0.0), axis=1, keepdims=True)


def waves(wave, cells, period):
    product = wave * cells
    left = product - jnp.floor(product * (1.0 / period)) * period
    left = jnp.where(left < 0.0, left + period, left)
    left = jnp.where(left >= period, left - period, left)
    quarter = jnp.floor(left * (4.0 / period) + 0.5)
    angle = (left - quarter * (period / 4.0)) * (2.0 * math.pi / period)
    square = angle * angle
    sine, cosine = 0.0, 0.0
    for k in (9, 7, 5, 3, 1):
        sine = sine * square + (-1.0) ** (k // 2) / math.factorial(k)
    for k in (10, 8, 6, 4, 2, 0):
        cosine = cosine * square + (-1.0) ** (k // 2) / math.factorial(k)
    sine = sine * angle
    odd = (quarter == 1.0) | (quarter == 3.0)
    cos_size, sin_size = jnp.where(odd, sine, cosine), jnp.where(odd, cosine, sine)
    cos_of = jnp.where((quarter == 1.0) | (quarter == 2.0), -cos_size, cos_size)
    sin_of = jnp.where((quarter == 2.0) | (quarter == 3.0), -sin_size, sin_size)
    return cos_of, sin_of


def split(table, parts):
    lead = table.astype(jnp.bfloat16)
    rest = (table - lead.astype(jnp.float32)).astype(jnp.bfloat16)
    return jnp.concatenate([(lead, rest)[part] for part in parts], axis=0)


def put_rows(state, f, t, part, values, parts):
    for b in range(values.shape[1] // LANES):
        spot = b * parts + part
        at = pl.ds(t * TILE + spot % TILE, TILE, stride=TILE)
        state[f, spot // TILE, at, :] = values[:, b * LANES : (b + 1) * LANES]


def prepare_kernel(
    lat_total, halves, place_ref, analysis_ref, zonal_hbm, meridional_hbm, code_hbm,
    state, added_ref, coef, table,
    own_ref, zonal_ref, meridional_ref, code_ref, lon_ref, lat_ref, sems,
):
    copies = [
        pltpu.make_async_copy(source, target, sems.at[i])
        for i, (source, target) in enumerate(
            (
                (zonal_hbm, zonal_ref),
                (meridional_hbm, meridional_ref),
                (code_hbm, code_ref),
                (analysis_ref, own_ref),
            )
        )
    ]
    for copy in copies:
        copy.start()
    levels, modes = zonal_ref.shape
    rows = own_ref.shape[2]
    half_rows = rows // halves
    length = half_rows + 2 * MARGIN
    lon_total, padded = lon_ref.shape[2], lat_ref.shape[2]
    start = place_ref[1] * rows - MARGIN

    table[...] = lon_operators()
    part = lax.broadcasted_iota(jnp.int32, (SUBS, LANES), 0) % halves
    row = start + part * half_rows + lax.broadcasted_iota(jnp.int32, (SUBS, LANES), 1)
    latitude = math.pi / 3.0 * (2.0 * (row.astype(jnp.float32) + 0.5) / lat_total - 1.0)
    factors = (
        (TIME_STEP / 12.0 / FILTER) / jnp.cos(latitude),
        (2.0 * TIME_STEP / FILTER) * jnp.sin(latitude),
        ((row >= 0) & (row < lat_total)).astype(jnp.float32),
    )
    for which in range(3):
        for t in range(length):
            tile = jnp.broadcast_to(factors[which][:TILE, t : t + 1], (TILE, LANES))
            for g in range(GROUPS):
                coef[which, g, t * TILE : (t + 1) * TILE, :] = tile

    lon_cells = lax.broadcasted_iota(jnp.int32, (modes, lon_total), 1).astype(jnp.float32)
    cell = lax.broadcasted_iota(jnp.int32, (modes, padded), 1) + start
    lat_cells = jnp.where((cell >= 0) & (cell < lat_total), cell, 0).astype(jnp.float32)
    cell = lax.broadcasted_iota(jnp.int32, (2 * modes, padded), 1) + start
    inside = (cell >= 0) & (cell < lat_total)
    for copy in copies[:3]:
        copy.wait()
    for l in range(levels):
        zonal, meridional, code = (
            as_column(r[l : l + 1, :].astype(jnp.float32)) for r in (zonal_ref, meridional_ref, code_ref)
        )
        weight = AMP_UNIT * code
        cos_of, sin_of = waves(zonal, lon_cells, lon_total)
        lon_ref[l] = split(jnp.concatenate([weight * cos_of, -weight * sin_of], axis=0), (0, 1, 0))
        cos_of, sin_of = waves(meridional, lat_cells, lat_total)
        lat_waves = jnp.concatenate([cos_of, sin_of], axis=0)
        lat_ref[l] = split(jnp.where(inside, lat_waves, 0.0), (0, 0, 1))

    copies[3].wait()

    def load(l, carry):
        added = lax.dot_general(
            lat_ref[l], lon_ref[l], (((0,), (0,)), ((), ())), preferred_element_type=jnp.float32
        )
        added_ref[l, :MARGIN, :] = added[:MARGIN]
        added_ref[l, MARGIN:, :] = added[rows + MARGIN : rows + 2 * MARGIN]
        for c in range(3):
            own = own_ref[c, l].astype(jnp.float32)
            if c == 0:
                own = (own + added[MARGIN : rows + MARGIN]).astype(jnp.bfloat16).astype(jnp.float32)
            for half in range(halves):
                for t in range(0, length, TILE):
                    at = half * half_rows + t - MARGIN
                    if 0 <= at < rows:
                        put_rows(state, c * levels + l, t, half, own[at : at + TILE], halves)
        return carry

    lax.fori_loop(0, levels, load, 0, unroll=True)


def member_kernel(levels, halves, blocks, rows, place_ref, outer_ref, inner_ref, added_ref, coef, table, _, *rest):
    outs, one, (two, ready) = rest[:-3], rest[-3], rest[-2:]
    half_rows = rows // halves
    length = half_rows + 2 * MARGIN
    odd = place_ref[0] == 1

    def load(l, carry):
        for c in range(3):
            inner, outer = (r[c, l].astype(jnp.float32) for r in (inner_ref, outer_ref))
            low, high = jnp.where(odd, inner, outer), jnp.where(odd, outer, inner)
            if c == 0:
                low = (low + added_ref[l, :MARGIN, :]).astype(jnp.bfloat16).astype(jnp.float32)
                high = (high + added_ref[l, MARGIN:, :]).astype(jnp.bfloat16).astype(jnp.float32)
            put_rows(one, c * levels + l, 0, 0, low, halves)
            put_rows(one, c * levels + l, length - MARGIN, halves - 1, high, halves)
        return carry

    lax.fori_loop(0, levels, load, 0)

    src, dst = one, two
    for step in range(STEPS):
        begin = 2 * (step + 1)
        count = length - 2 * begin

        group = group_of(count)

        def body(i, carry, src=src, dst=dst, begin=begin, group=group):
            step_rows(src, dst, coef, table, begin + i * group, group, halves, levels)
            return carry

        lax.fori_loop(0, count // group, body, 0)
        if step < STEPS - 1:
            @pl.when((place_ref[1] == 0) | (place_ref[1] == place_ref[2] - 1))
            def _(dst=dst, begin=begin):
                def clear(f, carry):
                    for t in list(range(begin, MARGIN)) + list(range(length - MARGIN, length - begin)):
                        at = slice(t * TILE, (t + 1) * TILE)
                        for g in range(GROUPS):
                            dst[f, g, at, :] = jnp.where(coef[2, g, at, :] > 0.5, dst[f, g, at, :], 0.0)
                    return carry

                lax.fori_loop(0, 3 * levels, clear, 0)
        src, dst = dst, src

    total = levels * rows
    per = len(outs)
    width = blocks * LANES // per
    for c in range(3):
        for b in range(blocks):
            tiles = []
            for l in range(levels):
                for half in range(halves):
                    for t in range(MARGIN, MARGIN + half_rows, TILE):
                        spot = b * halves + half
                        at = pl.ds(t * TILE + spot % TILE, TILE, stride=TILE)
                        tiles.append(src[c * levels + l, spot // TILE, at, :])
            for j in range(total // LANES):
                square = jnp.concatenate(tiles[j * (LANES // TILE) : (j + 1) * (LANES // TILE)], axis=0)
                turned = square.astype(jnp.bfloat16).T
                for d in range(LANES // width):
                    ready[b * (LANES // width) + d, c, :, j * LANES : (j + 1) * LANES] = turned[d * width : (d + 1) * width]
    for k in range(per):
        outs[k][...] = ready[place_ref[3 + k]]


def gather_kernel(levels, rows, place_ref, *refs):
    ins, (out_ref, held, laid, sems) = refs[:-4], refs[-4:]
    n = len(ins)
    copies = []
    for c in range(3):
        for k in range(n):
            held[place_ref[3 + k], c] = ins[k][c]
        for l in range(levels):
            laid[c, l] = jnp.concatenate([held[s, c, :, l * rows : (l + 1) * rows] for s in range(n)], axis=1)
            copies.append(pltpu.make_async_copy(laid.at[c, l], out_ref.at[c, l], sems.at[len(copies)]))
            copies[-1].start()
    for copy in copies:
        copy.wait()


def exchange_order(n):
    pairs = [(k, k + 1) for k in range(2, n, 2)]
    far = [p for p in reversed(pairs) if p[0] >= n // 2]
    near = [p for p in pairs if n // 4 <= p[0] < n // 2] + [p for p in reversed(pairs) if p[0] < n // 4]
    woven = far[:2]
    for k in range(max(len(far), len(near))):
        woven += near[k : k + 1] + far[k + 2 : k + 3]
    return [0] + [k for p in woven for k in p] + [1]


def shards(analysis, zonal_waves, meridional_waves, amplitude_codes):
    n = lax.axis_size("gx")
    place = lax.axis_index("gx")
    _, levels, rows, lon_total = analysis.shape
    lat_total = rows * n
    blocks = lon_total // LANES
    halves = SUBS // blocks
    half_rows = rows // halves
    length = half_rows + 2 * MARGIN
    width = lon_total // n
    total = levels * rows

    odd = place % 2
    first, last = analysis[:, :, :MARGIN], analysis[:, :, rows - MARGIN :]
    within = [(i, i ^ 1) for i in range(n)]
    between = [(i, ((i - 1) ^ 1) + 1) for i in range(1, n - 1)]
    inner = lax.ppermute(jnp.where(odd == 1, first, last), "gx", within)
    outer = lax.ppermute(jnp.where(odd == 1, last, first), "gx", between)

    order = exchange_order(n)
    partners = jnp.stack([place ^ k for k in order])
    scalars = jnp.concatenate([jnp.stack([odd, place, jnp.int32(n)]), partners]).astype(jnp.int32)

    vmem = pl.BlockSpec(memory_space=pltpu.VMEM)
    smem = pl.BlockSpec(memory_space=pltpu.SMEM)
    anywhere = pl.BlockSpec(memory_space=pltpu.HBM)
    padded = -(-(rows + 2 * MARGIN) // LANES) * LANES
    modes = zonal_waves.shape[1]
    state_shape = jax.ShapeDtypeStruct((3 * levels, GROUPS, length * TILE, LANES), jnp.float32)
    start, added, coef, table = pl.pallas_call(
        functools.partial(prepare_kernel, lat_total, halves),
        out_shape=[
            state_shape,
            jax.ShapeDtypeStruct((levels, 2 * MARGIN, lon_total), jnp.float32),
            jax.ShapeDtypeStruct((3, GROUPS, length * TILE, LANES), jnp.float32),
            jax.ShapeDtypeStruct((2 * LANES, 2 * LANES), jnp.bfloat16),
        ],
        in_specs=[smem] + [anywhere] * 4,
        out_specs=[vmem] * 4,
        scratch_shapes=[
            pltpu.VMEM(analysis.shape, jnp.bfloat16),
            pltpu.VMEM(zonal_waves.shape, jnp.int32),
            pltpu.VMEM(zonal_waves.shape, jnp.int32),
            pltpu.VMEM(zonal_waves.shape, jnp.int32),
            pltpu.VMEM((levels, 6 * modes, lon_total), jnp.bfloat16),
            pltpu.VMEM((levels, 6 * modes, padded), jnp.bfloat16),
            pltpu.SemaphoreType.DMA((4,)),
        ],
        cost_estimate=pl.CostEstimate(flops=4_000_000, bytes_accessed=8_000_000, transcendentals=80_000),
        compiler_params=pltpu.CompilerParams(vmem_limit_bytes=12 * 1024 * 1024),
        name="prepare",
    )(scalars, *(pltpu.with_memory_space_constraint(x, pltpu.HBM) for x in (analysis, zonal_waves, meridional_waves, amplitude_codes)))

    piece = jax.ShapeDtypeStruct((3, width, total), jnp.bfloat16)
    *sent, _ = pl.pallas_call(
        functools.partial(member_kernel, levels, halves, blocks, rows),
        out_shape=[piece] * n + [state_shape],
        in_specs=[smem] + [vmem] * 6,
        out_specs=[vmem] * (n + 1),
        input_output_aliases={6: n},
        scratch_shapes=[
            pltpu.VMEM((3 * levels, GROUPS, length * TILE, LANES), jnp.float32),
            pltpu.VMEM((n, 3, width, total), jnp.bfloat16),
        ],
        compiler_params=pltpu.CompilerParams(vmem_limit_bytes=16 * 1024 * 1024),
        name="member_steps",
    )(scalars, outer, inner, added, coef, table, start)

    got = [sent[0]]
    for piece_of, k in list(zip(sent, order))[1:]:
        got.append(lax.ppermute(piece_of, "gx", [(i, i ^ k) for i in range(n)]))
    return pl.pallas_call(
        functools.partial(gather_kernel, levels, rows),
        out_shape=jax.ShapeDtypeStruct((3, levels, width, lat_total), jnp.bfloat16),
        in_specs=[smem] + [vmem] * n,
        out_specs=pl.BlockSpec(memory_space=pl.ANY),
        scratch_shapes=[
            pltpu.VMEM((n, 3, width, total), jnp.bfloat16),
            pltpu.VMEM((3, levels, width, lat_total), jnp.bfloat16),
            pltpu.SemaphoreType.DMA((3 * levels,)),
        ],
        compiler_params=pltpu.CompilerParams(vmem_limit_bytes=12 * 1024 * 1024),
        name="lay_out",
    )(scalars, *got)


def solution(mesh):
    placed = (P(None, None, "gx", None), P("member", None), P("member", None), P("member", None))
    return jax.shard_map(
        shards, mesh=mesh, in_specs=placed, out_specs=P("member", None, "gx", None), check_vma=False
    )
```

```python
import functools
import math

import jax
import jax.numpy as jnp
from jax import lax
from jax.experimental import pallas as pl
from jax.experimental.pallas import tpu as pltpu
from jax.sharding import PartitionSpec as P

NY = 1536
STEPS = 4
TIME_STEP = 0.15
FILTER = 0.03
GRAVITY = 0.5
AMP_UNIT = 0.04
LANES = 128
SUBS = 16
TILE = 8
GROUPS = SUBS // TILE
MARGIN = 2 * STEPS


def lon_operators():
    shape = (2 * LANES, 2 * LANES)
    row = lax.broadcasted_iota(jnp.int32, shape, 0)
    column = lax.broadcasted_iota(jnp.int32, shape, 1)
    at = jnp.where(row < LANES + 2, row, jnp.where(row >= 2 * LANES - 2, row - 2 * LANES, -LANES))
    reach = at - jnp.where(column < LANES, column, column - LANES)
    size = jnp.abs(reach)
    slopes = jnp.where(size == 1, 8.0, jnp.where(size == 2, -1.0, 0.0)) * jnp.where(reach > 0, 1.0, -1.0)
    smooths = jnp.where(size == 0, -12.0, jnp.where(size == 1, 4.0, jnp.where(size == 2, -1.0, 0.0)))
    return jnp.where(column < LANES, slopes, smooths).astype(jnp.bfloat16)


def with_ends(x, halves, lane):
    ahead = pltpu.roll(x, SUBS - halves, 0)
    behind = pltpu.roll(x, halves, 0)
    return jnp.concatenate([x, jnp.where(lane < 2, ahead, behind)], axis=1)


def slope(p1, m1, p2, m2):
    return 8.0 * (p1 - m1) - (p2 - m2)


def level_sums(slopes):
    below = [None] * len(slopes)
    running = None
    for k in reversed(range(len(slopes))):
        running = slopes[k] if running is None else running + slopes[k]
        below[k] = running
    return [(0.5 * GRAVITY) * (running + b) for b in below]


def rows_of(ref, f, t):
    at = pl.ds(pl.multiple_of(t * TILE, TILE), TILE)
    return jnp.concatenate([ref[f, g, at, :] for g in range(GROUPS)], axis=0)


def step_rows(src, dst, coef, table, first, count, halves, levels):
    lane = lax.broadcasted_iota(jnp.int32, (SUBS, LANES), 1)
    gy = TIME_STEP / 12.0 / FILTER
    loaded = {}

    def get(f, k):
        if (f, k) not in loaded:
            loaded[f, k] = rows_of(src, f, first + k).astype(jnp.bfloat16)
        return loaded[f, k]

    flux = {}

    def north_flux(l, k):
        if (l, k) not in flux:
            v = get(2 * levels + l, k)
            flux[l, k] = v + get(l, k) * v
        return flux[l, k]

    def lon_parts(k):
        pieces = [with_ends(get(f, k), halves, lane) for f in range(3 * levels)]
        both = jnp.dot(jnp.concatenate(pieces, axis=0), table[...], preferred_element_type=jnp.float32)
        fluxes = []
        for l in range(levels):
            u = get(levels + l, k)
            fluxes.append(with_ends(u + get(l, k) * u, halves, lane))
        east = jnp.dot(jnp.concatenate(fluxes, axis=0), table[:, :LANES], preferred_element_type=jnp.float32)
        return both, east

    for k in range(count):
        t = first + k
        both, east_of = lon_parts(k)

        def parts(c, l):
            f = c * levels + l
            at = slice(f * SUBS, (f + 1) * SUBS)
            yp1, ym1, yp2, ym2 = (get(f, k + d) for d in (1, -1, 2, -2))
            ax = both[at, :LANES].astype(jnp.bfloat16)
            return ax, slope(yp1, ym1, yp2, ym2), 4.0 * (yp1 + ym1) - (yp2 + ym2), both[at, LANES:]

        def finish(c, l, smooth, change):
            f = c * levels + l
            change = smooth + change.astype(jnp.float32)
            new = rows_of(src, f, t) + FILTER * change
            at = pl.ds(pl.multiple_of(t * TILE, TILE), TILE)
            for g in range(GROUPS):
                dst[f, g, at, :] = new[g * TILE : (g + 1) * TILE]

        gx, gf = (rows_of(coef, i, t).astype(jnp.bfloat16) for i in range(2))
        hx, hy = [], []
        for l in range(levels):
            ax, ay, sy, sx = parts(0, l)
            hx.append(ax)
            hy.append(ay)
            east = east_of[l * SUBS : (l + 1) * SUBS].astype(jnp.bfloat16)
            north = slope(*(north_flux(l, k + d) for d in (1, -1, 2, -2)))
            finish(0, l, sx, sy - (gx * east + gy * north))
        px, py = level_sums(hx), level_sums(hy)
        for l in range(levels):
            u, v = get(levels + l, k), get(2 * levels + l, k)
            ax, ay, sy, sx = parts(1, l)
            finish(1, l, sx, sy - (gx * (u * ax + px[l]) + v * (gy * ay - gf)))
            ax, ay, sy, sx = parts(2, l)
            finish(2, l, sx, sy - (u * (gx * ax + gf) + gy * (v * ay + py[l])))


LARGEST_GROUP = 18


def group_of(count):
    return max(k for k in range(1, LARGEST_GROUP + 1) if count % k == 0)


def as_column(row):
    count = row.shape[1]
    square = jnp.broadcast_to(row, (count, count))
    here = lax.broadcasted_iota(jnp.int32, (count, count), 0) == lax.broadcasted_iota(jnp.int32, (count, count), 1)
    return jnp.sum(jnp.where(here, square, 0.0), axis=1, keepdims=True)


def waves(wave, cells, period):
    product = wave * cells
    left = product - jnp.floor(product * (1.0 / period)) * period
    left = jnp.where(left < 0.0, left + period, left)
    left = jnp.where(left >= period, left - period, left)
    quarter = jnp.floor(left * (4.0 / period) + 0.5)
    angle = (left - quarter * (period / 4.0)) * (2.0 * math.pi / period)
    square = angle * angle
    sine, cosine = 0.0, 0.0
    for k in (9, 7, 5, 3, 1):
        sine = sine * square + (-1.0) ** (k // 2) / math.factorial(k)
    for k in (10, 8, 6, 4, 2, 0):
        cosine = cosine * square + (-1.0) ** (k // 2) / math.factorial(k)
    sine = sine * angle
    odd = (quarter == 1.0) | (quarter == 3.0)
    cos_size, sin_size = jnp.where(odd, sine, cosine), jnp.where(odd, cosine, sine)
    cos_of = jnp.where((quarter == 1.0) | (quarter == 2.0), -cos_size, cos_size)
    sin_of = jnp.where((quarter == 2.0) | (quarter == 3.0), -sin_size, sin_size)
    return cos_of, sin_of


def split(table, parts):
    lead = table.astype(jnp.bfloat16)
    rest = (table - lead.astype(jnp.float32)).astype(jnp.bfloat16)
    return jnp.concatenate([(lead, rest)[part] for part in parts], axis=0)


def put_rows(state, f, t, part, values, parts):
    for b in range(values.shape[1] // LANES):
        spot = b * parts + part
        at = pl.ds(t * TILE + spot % TILE, TILE, stride=TILE)
        state[f, spot // TILE, at, :] = values[:, b * LANES : (b + 1) * LANES]


def prepare_kernel(
    lat_total, halves, place_ref, analysis_ref, zonal_hbm, meridional_hbm, code_hbm,
    state, added_ref, coef, table,
    own_ref, zonal_ref, meridional_ref, code_ref, lon_ref, lat_ref, sems,
):
    copies = [
        pltpu.make_async_copy(source, target, sems.at[i])
        for i, (source, target) in enumerate(
            (
                (zonal_hbm, zonal_ref),
                (meridional_hbm, meridional_ref),
                (code_hbm, code_ref),
                (analysis_ref, own_ref),
            )
        )
    ]
    for copy in copies:
        copy.start()
    levels, modes = zonal_ref.shape
    rows = own_ref.shape[2]
    half_rows = rows // halves
    length = half_rows + 2 * MARGIN
    lon_total, padded = lon_ref.shape[2], lat_ref.shape[2]
    start = place_ref[1] * rows - MARGIN

    table[...] = lon_operators()
    part = lax.broadcasted_iota(jnp.int32, (SUBS, LANES), 0) % halves
    row = start + part * half_rows + lax.broadcasted_iota(jnp.int32, (SUBS, LANES), 1)
    latitude = math.pi / 3.0 * (2.0 * (row.astype(jnp.float32) + 0.5) / lat_total - 1.0)
    factors = (
        (TIME_STEP / 12.0 / FILTER) / jnp.cos(latitude),
        (2.0 * TIME_STEP / FILTER) * jnp.sin(latitude),
        ((row >= 0) & (row < lat_total)).astype(jnp.float32),
    )
    for which in range(3):
        for t in range(length):
            tile = jnp.broadcast_to(factors[which][:TILE, t : t + 1], (TILE, LANES))
            for g in range(GROUPS):
                coef[which, g, t * TILE : (t + 1) * TILE, :] = tile

    lon_cells = lax.broadcasted_iota(jnp.int32, (modes, lon_total), 1).astype(jnp.float32)
    cell = lax.broadcasted_iota(jnp.int32, (modes, padded), 1) + start
    lat_cells = jnp.where((cell >= 0) & (cell < lat_total), cell, 0).astype(jnp.float32)
    cell = lax.broadcasted_iota(jnp.int32, (2 * modes, padded), 1) + start
    inside = (cell >= 0) & (cell < lat_total)
    for copy in copies[:3]:
        copy.wait()
    for l in range(levels):
        zonal, meridional, code = (
            as_column(r[l : l + 1, :].astype(jnp.float32)) for r in (zonal_ref, meridional_ref, code_ref)
        )
        weight = AMP_UNIT * code
        cos_of, sin_of = waves(zonal, lon_cells, lon_total)
        lon_ref[l] = split(jnp.concatenate([weight * cos_of, -weight * sin_of], axis=0), (0, 1, 0))
        cos_of, sin_of = waves(meridional, lat_cells, lat_total)
        lat_waves = jnp.concatenate([cos_of, sin_of], axis=0)
        lat_ref[l] = split(jnp.where(inside, lat_waves, 0.0), (0, 0, 1))

    copies[3].wait()

    def load(l, carry):
        added = lax.dot_general(
            lat_ref[l], lon_ref[l], (((0,), (0,)), ((), ())), preferred_element_type=jnp.float32
        )
        added_ref[l, :MARGIN, :] = added[:MARGIN]
        added_ref[l, MARGIN:, :] = added[rows + MARGIN : rows + 2 * MARGIN]
        for c in range(3):
            own = own_ref[c, l].astype(jnp.float32)
            if c == 0:
                own = (own + added[MARGIN : rows + MARGIN]).astype(jnp.bfloat16).astype(jnp.float32)
            for half in range(halves):
                for t in range(0, length, TILE):
                    at = half * half_rows + t - MARGIN
                    if 0 <= at < rows:
                        put_rows(state, c * levels + l, t, half, own[at : at + TILE], halves)
        return carry

    lax.fori_loop(0, levels, load, 0, unroll=True)


def member_kernel(levels, halves, blocks, rows, place_ref, inner_ref, outer_ref, added_ref, coef, table, _, *rest):
    outs, one, (two, ready) = rest[:-3], rest[-3], rest[-2:]
    half_rows = rows // halves
    length = half_rows + 2 * MARGIN
    odd = place_ref[0] == 1

    def load(l, carry):
        for c in range(3):
            inner, outer = (r[c, l].astype(jnp.float32) for r in (inner_ref, outer_ref))
            low, high = jnp.where(odd, inner, outer), jnp.where(odd, outer, inner)
            if c == 0:
                low = (low + added_ref[l, :MARGIN, :]).astype(jnp.bfloat16).astype(jnp.float32)
                high = (high + added_ref[l, MARGIN:, :]).astype(jnp.bfloat16).astype(jnp.float32)
            put_rows(one, c * levels + l, 0, 0, low, halves)
            put_rows(one, c * levels + l, length - MARGIN, halves - 1, high, halves)
        return carry

    lax.fori_loop(0, levels, load, 0)

    src, dst = one, two
    for step in range(STEPS):
        begin = 2 * (step + 1)
        count = length - 2 * begin

        group = group_of(count)

        def body(i, carry, src=src, dst=dst, begin=begin, group=group):
            step_rows(src, dst, coef, table, begin + i * group, group, halves, levels)
            return carry

        lax.fori_loop(0, count // group, body, 0)
        if step < STEPS - 1:
            @pl.when((place_ref[1] == 0) | (place_ref[1] == place_ref[2] - 1))
            def _(dst=dst, begin=begin):
                def clear(f, carry):
                    for t in list(range(begin, MARGIN)) + list(range(length - MARGIN, length - begin)):
                        at = slice(t * TILE, (t + 1) * TILE)
                        for g in range(GROUPS):
                            dst[f, g, at, :] = jnp.where(coef[2, g, at, :] > 0.5, dst[f, g, at, :], 0.0)
                    return carry

                lax.fori_loop(0, 3 * levels, clear, 0)
        src, dst = dst, src

    total = levels * rows
    per = len(outs)
    width = blocks * LANES // per
    for c in range(3):
        for b in range(blocks):
            tiles = []
            for l in range(levels):
                for half in range(halves):
                    for t in range(MARGIN, MARGIN + half_rows, TILE):
                        spot = b * halves + half
                        at = pl.ds(t * TILE + spot % TILE, TILE, stride=TILE)
                        tiles.append(src[c * levels + l, spot // TILE, at, :])
            for j in range(total // LANES):
                square = jnp.concatenate(tiles[j * (LANES // TILE) : (j + 1) * (LANES // TILE)], axis=0)
                turned = square.astype(jnp.bfloat16).T
                for d in range(LANES // width):
                    ready[b * (LANES // width) + d, c, :, j * LANES : (j + 1) * LANES] = turned[d * width : (d + 1) * width]
    for k in range(per):
        outs[k][...] = ready[place_ref[3 + k]]


def gather_kernel(levels, rows, place_ref, *refs):
    ins, (out_ref, held, laid, sems) = refs[:-4], refs[-4:]
    n = len(ins)
    copies = []
    for c in range(3):
        for k in range(n):
            held[place_ref[3 + k], c] = ins[k][c]
        for l in range(levels):
            laid[c, l] = jnp.concatenate([held[s, c, :, l * rows : (l + 1) * rows] for s in range(n)], axis=1)
            copies.append(pltpu.make_async_copy(laid.at[c, l], out_ref.at[c, l], sems.at[len(copies)]))
            copies[-1].start()
    for copy in copies:
        copy.wait()


def exchange_order(n):
    pairs = [(k, k + 1) for k in range(2, n, 2)]
    far = [p for p in reversed(pairs) if p[0] >= n // 2]
    near = [p for p in pairs if n // 4 <= p[0] < n // 2] + [p for p in reversed(pairs) if p[0] < n // 4]
    woven = far[:3]
    for k in range(max(len(far), len(near))):
        woven += near[k : k + 1] + far[k + 3 : k + 4]
    return [0] + [k for p in woven for k in p] + [1]


def shards(analysis, zonal_waves, meridional_waves, amplitude_codes):
    n = lax.axis_size("gx")
    place = lax.axis_index("gx")
    _, levels, rows, lon_total = analysis.shape
    lat_total = rows * n
    blocks = lon_total // LANES
    halves = SUBS // blocks
    half_rows = rows // halves
    length = half_rows + 2 * MARGIN
    width = lon_total // n
    total = levels * rows

    odd = place % 2
    first, last = analysis[:, :, :MARGIN], analysis[:, :, rows - MARGIN :]
    within = [(i, i ^ 1) for i in range(n)]
    between = [(i, ((i - 1) ^ 1) + 1) for i in range(1, n - 1)]
    inner = lax.ppermute(jnp.where(odd == 1, first, last), "gx", within)
    outer = lax.ppermute(jnp.where(odd == 1, last, first), "gx", between)

    order = exchange_order(n)
    partners = jnp.stack([place ^ k for k in order])
    scalars = jnp.concatenate([jnp.stack([odd, place, jnp.int32(n)]), partners]).astype(jnp.int32)

    vmem = pl.BlockSpec(memory_space=pltpu.VMEM)
    smem = pl.BlockSpec(memory_space=pltpu.SMEM)
    anywhere = pl.BlockSpec(memory_space=pltpu.HBM)
    padded = -(-(rows + 2 * MARGIN) // LANES) * LANES
    modes = zonal_waves.shape[1]
    state_shape = jax.ShapeDtypeStruct((3 * levels, GROUPS, length * TILE, LANES), jnp.float32)
    start, added, coef, table = pl.pallas_call(
        functools.partial(prepare_kernel, lat_total, halves),
        out_shape=[
            state_shape,
            jax.ShapeDtypeStruct((levels, 2 * MARGIN, lon_total), jnp.float32),
            jax.ShapeDtypeStruct((3, GROUPS, length * TILE, LANES), jnp.float32),
            jax.ShapeDtypeStruct((2 * LANES, 2 * LANES), jnp.bfloat16),
        ],
        in_specs=[smem] + [anywhere] * 4,
        out_specs=[vmem] * 4,
        scratch_shapes=[
            pltpu.VMEM(analysis.shape, jnp.bfloat16),
            pltpu.VMEM(zonal_waves.shape, jnp.int32),
            pltpu.VMEM(zonal_waves.shape, jnp.int32),
            pltpu.VMEM(zonal_waves.shape, jnp.int32),
            pltpu.VMEM((levels, 6 * modes, lon_total), jnp.bfloat16),
            pltpu.VMEM((levels, 6 * modes, padded), jnp.bfloat16),
            pltpu.SemaphoreType.DMA((4,)),
        ],
        cost_estimate=pl.CostEstimate(flops=4_000_000, bytes_accessed=8_000_000, transcendentals=80_000),
        compiler_params=pltpu.CompilerParams(vmem_limit_bytes=12 * 1024 * 1024),
        name="prepare",
    )(scalars, *(pltpu.with_memory_space_constraint(x, pltpu.HBM) for x in (analysis, zonal_waves, meridional_waves, amplitude_codes)))

    piece = jax.ShapeDtypeStruct((3, width, total), jnp.bfloat16)
    *sent, _ = pl.pallas_call(
        functools.partial(member_kernel, levels, halves, blocks, rows),
        out_shape=[piece] * n + [state_shape],
        in_specs=[smem] + [vmem] * 6,
        out_specs=[vmem] * (n + 1),
        input_output_aliases={6: n},
        scratch_shapes=[
            pltpu.VMEM((3 * levels, GROUPS, length * TILE, LANES), jnp.float32),
            pltpu.VMEM((n, 3, width, total), jnp.bfloat16),
        ],
        compiler_params=pltpu.CompilerParams(vmem_limit_bytes=16 * 1024 * 1024),
        name="member_steps",
    )(scalars, inner, outer, added, coef, table, start)

    got = [sent[0]]
    for piece_of, k in list(zip(sent, order))[1:]:
        got.append(lax.ppermute(piece_of, "gx", [(i, i ^ k) for i in range(n)]))
    return pl.pallas_call(
        functools.partial(gather_kernel, levels, rows),
        out_shape=jax.ShapeDtypeStruct((3, levels, width, lat_total), jnp.bfloat16),
        in_specs=[smem] + [vmem] * n,
        out_specs=pl.BlockSpec(memory_space=pl.ANY),
        scratch_shapes=[
            pltpu.VMEM((n, 3, width, total), jnp.bfloat16),
            pltpu.VMEM((3, levels, width, lat_total), jnp.bfloat16),
            pltpu.SemaphoreType.DMA((3 * levels,)),
        ],
        compiler_params=pltpu.CompilerParams(vmem_limit_bytes=12 * 1024 * 1024),
        name="lay_out",
    )(scalars, *got)


def solution(mesh):
    placed = (P(None, None, "gx", None), P("member", None), P("member", None), P("member", None))
    return jax.shard_map(
        shards, mesh=mesh, in_specs=placed, out_specs=P("member", None, "gx", None), check_vma=False
    )
```
